32 devices in a mesh: dp: 8 (over z, x), tensor: 4 (over y, core).
Axes of the slice: x: 2, y: 2, z: 4, core: 2. Of those that a mesh axis runs over, the one named last changes fastest.
Arguments:
- text_embed: bfloat16 [32, 384, 768], P('dp'), may hold values from -6 to 6
- region_feats: bfloat16 [3072, 2048], P('dp', 'tensor'), may hold values from -6 to 6
- box_coords: int32 [3072, 4], P('dp'), may hold values from 0 to 127
- seg_ids: int32 [32, 512], P('dp'), may hold values from 0 to 5, never falling along the last dimension, each value on 1 to 256 neighbouring positions
- region_counts: int32 [32], P('dp'), may hold values from 1 to 128, as said below
- send_index: int32 [8, 8, 96], P('dp'), may hold values from -1 to 383, as said below
- recv_pos: int32 [8, 8, 96], P('dp'), may hold values from -1 to 2047, as said below
- w_proj: bfloat16 [2048, 768], P('tensor'), may hold values from -0.125 to 0.125
- box_table: bfloat16 [4, 128, 768], replicated, may hold values from -1.75 to 1.75
- type_embed: bfloat16 [2, 768], replicated, may hold values from -3 to 3
- pos_embed: bfloat16 [512, 768], replicated, may hold values from -3 to 3
- gain_embed: float32 [768], replicated, may hold values from 0.5 to 1.5
- bias_embed: float32 [768], replicated, may hold values from -1.75 to 1.75
- w_qkv: bfloat16 [3, 768, 768], P(None, None, 'tensor'), may hold values from -0.21875 to 0.21875
- w_mix: bfloat16 [768, 768], P('tensor'), may hold values from -1.75 to 1.75
- gain_mid: float32 [768], replicated, may hold values from 0.5 to 1.5
- bias_mid: float32 [768], replicated, may hold values from -1.75 to 1.75
- w_up: bfloat16 [768, 3072], P(None, 'tensor'), may hold values from -0.21875 to 0.21875
- w_down: bfloat16 [3072, 768], P('tensor'), may hold values from -0.15625 to 0.15625
- gain_final: float32 [768], replicated, may hold values from 0.5 to 1.5
- bias_final: float32 [768], replicated, may hold values from -1.75 to 1.75
- cotangent: bfloat16 [32, 512, 768], P('dp'), may hold values from -8 to 8
Outputs:
- layer_output: bfloat16 [32, 512, 768], P('dp')
- text_grad: float32 [32, 384, 768], P('dp')
- feat_grad: float32 [3072, 2048], P('dp', 'tensor')
- grad_proj: float32 [2048, 768], P('tensor', 'dp')
- grad_box: float32 [4, 128, 768], P(None, 'dp')
- grad_type: float32 [2, 768], P(None, 'dp')
- grad_pos: float32 [512, 768], P('dp')
- grad_gain_embed: float32 [768], P('dp')
- grad_bias_embed: float32 [768], P('dp')
- grad_qkv: float32 [3, 768, 768], P(None, 'dp', 'tensor')
- grad_mix: float32 [768, 768], P('tensor', 'dp')
- grad_gain_mid: float32 [768], P('dp')
- grad_bias_mid: float32 [768], P('dp')
- grad_up: float32 [768, 3072], P('dp', 'tensor')
- grad_down: float32 [3072, 768], P('tensor', 'dp')
- grad_gain_final: float32 [768], P('dp')
- grad_bias_final: float32 [768], P('dp')
The draws below stay inside these ranges and needn't reach their ends.
Inputs may be any that keep to these rules, and one draw needn't show every extreme that they name: `seg_ids`: each row holds 6 documents; ids never fall along a row. `region_counts`: the 4 rows of each device hold 384 regions in all, and one of them holds 128. `send_index`: entry [s, d, c] is the index, among device s's 384 stored regions, of the c-th region that device s sends to device d, or -1; every stored region is named once; for each pair the named entries come first and are even in number, at most 96, and every device sends exactly 96 to some device. `recv_pos`: entry [d, s, c] is the token, among device d's 4 * 512 tokens numbered row by row, that receives the region named by send_index[s, d, c], and -1 exactly where that entry is -1; the tokens named are the region tokens of device d's rows, position 384 + q of a row with q below its region count, each once.
All inputs are finite; a program needn't handle non-finite values.
Results may differ from the reference program's by a relative error of at most 0.03.
Values may be sent and summed in bfloat16 or wider, within the bound.
No kernel may reach another device: no remote copies, remote signals or barrier semaphores. Data moves between devices by JAX's collectives and lax.ppermute only.
A program may use at most 192 MiB of HBM per device.

```python
import math
import jax
import jax.numpy as jnp
import numpy as np
from jax import lax

D = 768
HEADS = 12
HD = 64
FF = 3072
FV = 2048
L = 512
RMAX = 128
LT = 384
QB = 128
DOCS = 6
ROWS_DEV = 4
REG = 384
PEERS = 8
CAP = 96
NROWS = 32
NREG = 3072
N_TENSOR = 4


def route_tables(key):
    base = jax.random.fold_in(key, 7001)
    keys = jax.random.split(base, 7)
    peers = 2 * REG // CAP
    most = CAP // 2
    half = REG // 2
    tickets = jnp.arange(REG, dtype=jnp.int32) // most
    forced = jax.random.randint(keys[0], (), 0, peers, dtype=jnp.int32)
    ranks = jax.random.permutation(keys[1], REG).astype(jnp.int32)
    scores = ranks + jnp.where(tickets == forced, -REG, 0).astype(jnp.int32)
    chosen = jnp.argsort(scores)[:half]
    offsets = tickets[chosen]
    relabel = jax.random.permutation(keys[2], peers).astype(jnp.int32)
    shifts = jax.random.permutation(keys[3], peers).astype(jnp.int32)
    places = jnp.arange(half, dtype=jnp.int32)
    devices = jnp.arange(peers, dtype=jnp.int32)

    def sender(source):
        dests = relabel[(shifts[source] + offsets) % peers]
        order = jnp.argsort(dests * half + places)
        sorted_dest = dests[order]
        per_dest = jnp.sum((dests[None, :] == devices[:, None]).astype(jnp.int32), axis=1)
        first = jnp.cumsum(per_dest) - per_dest
        within = places - first[sorted_dest]
        shuffle = jax.random.permutation(jax.random.fold_in(keys[4], source), REG).astype(jnp.int32)
        table = jnp.full((peers, CAP), -1, jnp.int32)
        table = table.at[sorted_dest, 2 * within].set(shuffle[2 * places])
        table = table.at[sorted_dest, 2 * within + 1].set(shuffle[2 * places + 1])
        return table
    sends = jax.vmap(sender)(devices)
    spare = REG - RMAX - (ROWS_DEV - 1)
    slots = (ROWS_DEV - 1) * (RMAX - 1)
    owner = jnp.arange(slots, dtype=jnp.int32) // (RMAX - 1)
    rows = jnp.arange(ROWS_DEV, dtype=jnp.int32)

    def count_rows(device):
        local = jax.random.fold_in(keys[5], device)
        first_key, second_key = jax.random.split(local)
        full_row = jax.random.randint(first_key, (), 0, ROWS_DEV, dtype=jnp.int32)
        picked = jax.random.permutation(second_key, slots).astype(jnp.int32) < spare
        others = 1 + jnp.sum(((owner[None, :] == rows[:ROWS_DEV - 1, None]) & picked[None, :]).astype(jnp.int32), axis=1)
        shifted = jnp.clip(rows - (rows > full_row).astype(jnp.int32), 0, ROWS_DEV - 2)
        return jnp.where(rows == full_row, RMAX, others[shifted]).astype(jnp.int32)
    counts = jax.vmap(count_rows)(devices)
    slot_q = jnp.arange(RMAX, dtype=jnp.int32)
    candidates = (rows[:, None] * L + LT + slot_q[None, :]).reshape(-1)
    cand_index = jnp.arange(ROWS_DEV * RMAX, dtype=jnp.int32)

    def receiver(device):
        usable = (slot_q[None, :] < counts[device][:, None]).reshape(-1)
        order = jnp.argsort(jnp.where(usable, cand_index, cand_index + ROWS_DEV * RMAX))
        spots = candidates[order][:REG]
        spots = spots[jax.random.permutation(jax.random.fold_in(keys[6], device), REG).astype(jnp.int32)]
        incoming = sends[:, device, :]
        filled = (incoming >= 0).reshape(-1)
        rank = jnp.cumsum(filled.astype(jnp.int32)) - 1
        return jnp.where(filled, spots[jnp.clip(rank, 0, REG - 1)], -1).astype(jnp.int32).reshape(peers, CAP)
    receives = jax.vmap(receiver)(devices)
    return (counts.reshape(-1), sends, receives)


def draw_region_counts(key, part):
    return route_tables(key)[0]


def draw_send_index(key, part):
    return route_tables(key)[1]


def draw_recv_pos(key, part):
    return route_tables(key)[2]


def set_ends(entries, own_key, least, high):
    dims = entries.shape
    place = [jax.random.randint(jax.random.fold_in(own_key, axis), (), 0, dims[axis]) for axis in range(len(dims))]
    entries = entries.at[tuple(place)].set(least)
    longest = dims.index(max(dims))
    place[longest] = (place[longest] + 1) % dims[longest]
    return entries.at[tuple(place)].set(high)


def spiked(values, rng, source, target, blocks, factor):
    def block_of(dim):
        return (jnp.arange(values.shape[dim]) // (values.shape[dim] // blocks)).reshape((-1,) + (1,) * (values.ndim - 1 - dim))

    first = jax.random.permutation(rng, blocks)[block_of(target)]
    far = (block_of(target) + blocks // 2) % blocks
    return jnp.where((block_of(source) == first) | (block_of(source) == far), factor * values, values)


def steps_of(rng, shape, pieces, smallest, top_value):
    def one(position, shards_of):
        draws = jax.random.uniform(jax.random.fold_in(jax.random.fold_in(rng, 6), position), (shards_of,), jnp.float32, smallest / len(pieces), top_value / len(pieces))
        return jnp.repeat(jnp.exp(draws), shape[position] // shards_of).reshape((-1,) + (1,) * (len(shape) - position - 1))

    level = one(*pieces[0])
    for cut in pieces[1:]:
        level = level * one(*cut)
    return level


def split_up(count, total, bound, skew):
    portions = [(1 << 20) // math.isqrt(standing ** skew) + 1 for standing in range(2, count + 1)]
    rest, holding = total - bound - (count - 1), [1] * (count - 1)
    while rest > 0:
        free = [i for i in range(count - 1) if holding[i] < bound]
        pool, remaining = sum([portions[i] for i in free]), rest
        for i in free:
            extra = min(bound - holding[i], max(1, remaining * portions[i] // pool), rest)
            holding[i] = holding[i] + extra
            rest = rest - extra
    return np.array([bound] + holding)


def uneven_parts(rng, count, total, reach, lean):
    if count == 2:
        one = jax.random.randint(rng, (), max(1, total - reach), min(reach, total - 1) + 1)
        return jnp.stack([one, total - one])
    sizes = jnp.asarray(split_up(count, total, reach, lean), jnp.int32)
    couples = (count - 1) // 2
    source_of, taker = sizes[1:1 + 2 * couples:2], sizes[2:2 + 2 * couples:2]
    room = jnp.minimum(source_of - 1, reach - taker)
    moved = jax.random.randint(jax.random.fold_in(rng, 1), (couples,), 0, 1 << 20) % (room + 1)
    sizes = sizes.at[1:1 + 2 * couples:2].set(source_of - moved).at[2:2 + 2 * couples:2].set(taker + moved)
    return sizes[jax.random.permutation(jax.random.fold_in(rng, 2), count)]


def scatter_about(key, dims, deviation, reach, cuts=(), held_as=jnp.bfloat16):
    result = deviation * jax.random.normal(key, dims, jnp.float32)
    if cuts:
        result = result * steps_of(key, dims, cuts, -0.22, 0.18)
    return jnp.clip(result, -reach, reach).astype(held_as)


def heavy_noise(key, dims, scale, most, cuts, heavy, kind=jnp.bfloat16):
    drawn = scale * jax.random.normal(key, dims, jnp.float32)
    if cuts:
        drawn = drawn * steps_of(key, dims, cuts, -0.22, 0.18)
    return jnp.clip(spiked(drawn, jax.random.fold_in(key, 3), *heavy), -most, most).astype(kind)


def setup_inputs(seed: int = 0) -> dict:
    arg_keys = jax.random.split(jax.random.key(seed), 23)
    return {
        "text_embed": scatter_about(arg_keys[0], (NROWS, LT, D), 1.0, 6.0, ((0, 8),)),
        "region_feats": scatter_about(arg_keys[1], (NREG, FV), 1.0, 6.0, ((0, 8), (1, 4))),
        "box_coords": set_ends(jax.random.randint(arg_keys[2], (NREG, 4), 0, QB), jax.random.fold_in(arg_keys[2], 1), 0, QB - 1).astype(jnp.int32),
        "seg_ids": jax.vmap(lambda own: jnp.searchsorted(jnp.cumsum(uneven_parts(own, DOCS, L, L // 2, 1)), jnp.arange(L), side="right"))(jax.random.split(arg_keys[3], NROWS)).reshape((NROWS, L)).astype(jnp.int32),
        "region_counts": draw_region_counts(jax.random.fold_in(arg_keys[22], 71), 0),
        "send_index": draw_send_index(jax.random.fold_in(arg_keys[22], 71), 0),
        "recv_pos": draw_recv_pos(jax.random.fold_in(arg_keys[22], 71), 0),
        "w_proj": scatter_about(arg_keys[7], (FV, D), FV ** -0.5, 0.125, ((0, 4),)),
        "box_table": scatter_about(arg_keys[8], (4, QB, D), 0.3, 1.75),
        "type_embed": scatter_about(arg_keys[9], (2, D), 0.5, 3.0),
        "pos_embed": scatter_about(arg_keys[10], (L, D), 0.5, 3.0),
        "gain_embed": jnp.clip(1.0 + 0.1 * jax.random.normal(arg_keys[11], (D,), jnp.float32), 0.5, 1.5),
        "bias_embed": scatter_about(arg_keys[12], (D,), 0.3, 1.75, (), jnp.float32),
        "w_qkv": scatter_about(arg_keys[13], (3, D, D), D ** -0.5, 0.21875, ((2, 4),)),
        "w_mix": scatter_about(arg_keys[14], (D, D), (D // 64) ** -0.5, 1.75, ((0, 4),)),
        "gain_mid": jnp.clip(1.0 + 0.1 * jax.random.normal(arg_keys[15], (D,), jnp.float32), 0.5, 1.5),
        "bias_mid": scatter_about(arg_keys[16], (D,), 0.3, 1.75, (), jnp.float32),
        "w_up": scatter_about(arg_keys[17], (D, FF), D ** -0.5, 0.21875, ((1, 4),)),
        "w_down": scatter_about(arg_keys[18], (FF, D), (FF // 2) ** -0.5, 0.15625, ((0, 4),)),
        "gain_final": jnp.clip(1.0 + 0.1 * jax.random.normal(arg_keys[19], (D,), jnp.float32), 0.5, 1.5),
        "bias_final": scatter_about(arg_keys[20], (D,), 0.3, 1.75, (), jnp.float32),
        "cotangent": heavy_noise(arg_keys[21], (NROWS, L, D), 1.0, 8.0, ((0, 8),), (0, 2, 8, 2.0)),
    }


EPSILON = 1e-06
NEGATIVE = -1000000000.0
HIGH = lax.Precision.HIGHEST

@jax.custom_vjp
def low(v):
    return lax.optimization_barrier(v.astype(jnp.bfloat16)).astype(jnp.float32)

@jax.custom_vjp
def low_back(v):
    return v

def low_keep(v):
    return (low(v), None)

def low_pass(kept, grad):
    return (grad,)

def back_keep(v):
    return (v, None)

def back_low(kept, grad):
    return (low(grad),)
low.defvjp(low_keep, low_pass)
low_back.defvjp(back_keep, back_low)

def layer_norm(values, gain, bias):
    mean = lax.optimization_barrier(jnp.mean(values, axis=-1, keepdims=True))
    centred = values - mean
    variance = lax.optimization_barrier(jnp.mean(centred * centred, axis=-1, keepdims=True))
    return centred * lax.rsqrt(variance + EPSILON) * gain + bias

def key_mask(seg_row, count):
    places = jnp.arange(L, dtype=jnp.int32)
    usable = places < LT + count
    same = seg_row[:, None] == seg_row[None, :]
    return same & (usable[None, :] | (places[:, None] == places[None, :]))

def attend(queries, keys, values, seg_row, count):
    scores = jnp.einsum('qhd,khd->hqk', queries, keys, precision=HIGH) * HD ** (-0.5)
    scores = low_back(scores)
    allowed = key_mask(seg_row, count)
    scores = jnp.where(allowed[None], scores, NEGATIVE)
    probs = jax.nn.softmax(scores, axis=-1)
    return jnp.einsum('hqk,khd->qhd', low(probs), values, precision=HIGH)

def reference(text_embed, region_feats, box_coords, seg_ids, region_counts, send_index, recv_pos, w_proj, box_table, type_embed, pos_embed, gain_embed, bias_embed, w_qkv, w_mix, gain_mid, bias_mid, w_up, w_down, gain_final, bias_final, cotangent):
    send_turned = jnp.transpose(send_index, (1, 0, 2))
    global_region = jnp.arange(PEERS, dtype=jnp.int32)[None, :, None] * REG + send_turned
    global_token = jnp.arange(PEERS, dtype=jnp.int32)[:, None, None] * (ROWS_DEV * L) + recv_pos
    spots = jnp.where(recv_pos >= 0, global_token, PEERS * ROWS_DEV * L).reshape(-1).astype(jnp.int32)
    token_region = jnp.full((PEERS * ROWS_DEV * L,), -1, jnp.int32).at[spots].set(global_region.reshape(-1).astype(jnp.int32), mode='drop')
    floats = (text_embed, region_feats, w_proj, box_table, type_embed, pos_embed, gain_embed, bias_embed, w_qkv, w_mix, gain_mid, bias_mid, w_up, w_down, gain_final, bias_final)
    floats = tuple((item.astype(jnp.float32) for item in floats))

    def forward(text_embed, region_feats, w_proj, box_table, type_embed, pos_embed, gain_embed, bias_embed, w_qkv, w_mix, gain_mid, bias_mid, w_up, w_down, gain_final, bias_final):
        region_proj = jnp.dot(region_feats, w_proj, precision=HIGH)
        boxed = box_table[0][box_coords[:, 0]] + box_table[1][box_coords[:, 1]] + box_table[2][box_coords[:, 2]] + box_table[3][box_coords[:, 3]]
        region_rows = low_back(low(region_proj + boxed))
        groups = (text_embed.reshape(PEERS, ROWS_DEV, LT, D), token_region.reshape(PEERS, ROWS_DEV * L), seg_ids.reshape(PEERS, ROWS_DEV, L), region_counts.reshape(PEERS, ROWS_DEV))
        width = D // N_TENSOR
        group_heads = HEADS // N_TENSOR
        inner = FF // N_TENSOR

        def group_step(carry, group):
            text_rows, region_map, seg_rows, count_rows = group
            gathered = jnp.where((region_map >= 0)[:, None], region_rows[jnp.maximum(region_map, 0)], 0.0)
            is_text = (jnp.arange(L, dtype=jnp.int32) < LT)[:, None]
            typed = jnp.where(is_text, type_embed[0][None, :], type_embed[1][None, :])
            padded_text = jnp.concatenate([text_rows, jnp.zeros((ROWS_DEV, L - LT, D), jnp.float32)], axis=1)
            embedded = gathered.reshape(ROWS_DEV, L, D) + padded_text + typed[None] + pos_embed[None]
            hidden0 = layer_norm(embedded, gain_embed, bias_embed).reshape(ROWS_DEV * L, D)
            shared0 = low(hidden0)
            attn = jnp.zeros((ROWS_DEV * L, D), jnp.float32)
            for shard in range(N_TENSOR):
                inputs = low_back(shared0)
                mixed = jnp.einsum('td,cde->cte', inputs, w_qkv[:, :, shard * width:(shard + 1) * width], precision=HIGH)
                mixed = low_back(low(mixed)).reshape(3, ROWS_DEV, L, group_heads, HD)
                context = jax.vmap(attend)(mixed[0], mixed[1], mixed[2], seg_rows, count_rows)
                context = low_back(low(context.reshape(ROWS_DEV * L, width)))
                attn = attn + low(jnp.dot(context, w_mix[shard * width:(shard + 1) * width], precision=HIGH))
            attn = low_back(attn)
            hidden1 = layer_norm(hidden0 + attn, gain_mid, bias_mid)
            shared1 = low(hidden1)
            ffn = jnp.zeros((ROWS_DEV * L, D), jnp.float32)
            for shard in range(N_TENSOR):
                inputs = low_back(shared1)
                before = low_back(jnp.dot(inputs, w_up[:, shard * inner:(shard + 1) * inner], precision=HIGH))
                active = low(jax.nn.gelu(before, approximate=False))
                ffn = ffn + low(jnp.dot(active, w_down[shard * inner:(shard + 1) * inner], precision=HIGH))
            ffn = low_back(ffn)
            final = layer_norm(hidden1 + ffn, gain_final, bias_final)
            return (carry, final.reshape(ROWS_DEV, L, D))
        _, finals = lax.scan(jax.checkpoint(group_step), jnp.zeros((), jnp.float32), groups)
        return finals
    finals, pullback = jax.vjp(forward, *floats)
    grads = pullback(cotangent.astype(jnp.float32).reshape(PEERS, ROWS_DEV, L, D))
    layer_output = finals.reshape(PEERS * ROWS_DEV, L, D).astype(jnp.bfloat16)
    return (layer_output, grads[0], grads[1], grads[2], grads[3], grads[4], grads[5], grads[6], grads[7], grads[8], grads[9], grads[10], grads[11], grads[12], grads[13], grads[14], grads[15])
```

```python
import jax
import jax.numpy as jnp
from jax import lax
from jax.sharding import PartitionSpec as P

HD = 64
LT = 384
EPSILON = 1e-06
NEGATIVE = -1000000000.0
BF = jnp.bfloat16
F32 = jnp.float32


def layer_norm(values, gain, bias):
    mean = jnp.mean(values, axis=-1, keepdims=True)
    centred = values - mean
    variance = jnp.mean(centred * centred, axis=-1, keepdims=True)
    inverse = lax.rsqrt(variance + EPSILON)
    normed = centred * inverse
    return (normed * gain + bias, normed, inverse)


def norm_back(grad, normed, inverse, gain):
    scaled = grad * gain
    mean_grad = jnp.mean(scaled, axis=-1, keepdims=True)
    mean_proj = jnp.mean(scaled * normed, axis=-1, keepdims=True)
    grad_in = inverse * (scaled - mean_grad - normed * mean_proj)
    return (grad_in, jnp.sum(grad * normed, axis=0), jnp.sum(grad, axis=0))


def key_mask(seg_row, count):
    length = seg_row.shape[0]
    places = jnp.arange(length, dtype=jnp.int32)
    usable = places < LT + count
    same = seg_row[:, None] == seg_row[None, :]
    return same & (usable[None, :] | (places[:, None] == places[None, :]))


def masked_scores(queries, keys, allowed):
    scale = queries.shape[-1] ** (-0.5)
    scores = jnp.einsum("qhd,khd->hqk", queries, keys, preferred_element_type=F32) * scale
    return jnp.where(allowed[None], scores, NEGATIVE)


def attend(queries, keys, values, allowed):
    scores = masked_scores(queries, keys, allowed)
    top = jnp.max(scores, axis=-1, keepdims=True)
    total = jnp.sum(jnp.exp(scores - top), axis=-1, keepdims=True)
    logsum = top + jnp.log(total)
    probs = jnp.exp(scores - logsum)
    context = jnp.einsum("hqk,khd->qhd", probs.astype(BF), values, preferred_element_type=F32)
    return (context.astype(BF), logsum)


def attend_back(queries, keys, values, grad_context, logsum, allowed):
    scale = queries.shape[-1] ** (-0.5)
    scores = masked_scores(queries, keys, allowed)
    probs = jnp.exp(scores - logsum)
    grad_probs = jnp.einsum("qhd,khd->hqk", grad_context, values, preferred_element_type=F32)
    inner = jnp.sum(probs * grad_probs, axis=-1, keepdims=True)
    grad_scores = (probs * (grad_probs - inner)).astype(BF)
    grad_queries = (
        jnp.einsum("hqk,khd->qhd", grad_scores, keys, preferred_element_type=F32) * scale
    ).astype(BF)
    grad_keys = (
        jnp.einsum("hqk,qhd->khd", grad_scores, queries, preferred_element_type=F32) * scale
    ).astype(BF)
    grad_values = jnp.einsum(
        "hqk,qhd->khd", probs.astype(BF), grad_context, preferred_element_type=F32
    ).astype(BF)
    return (grad_queries, grad_keys, grad_values)


def swap(value, axis, bit):
    count = lax.axis_size(axis)
    return lax.ppermute(value, axis, [(i, i ^ bit) for i in range(count)])


def bits_of(axis):
    count = lax.axis_size(axis)
    return [1 << i for i in range(count.bit_length() - 1)]


def gather_shards(shard):
    held = {0: shard}
    for bit in reversed(bits_of("tensor")):
        held.update({k | bit: swap(v, "tensor", bit) for k, v in list(held.items())})
    return [held[k] for k in sorted(held)]


def reduce_shards(parts):
    held = dict(enumerate(parts))
    for bit in bits_of("tensor"):
        moved = {k: swap(v.astype(BF), "tensor", bit) for k, v in held.items() if k & bit}
        held = {
            k: v + moved[k | bit].astype(F32) for k, v in held.items() if not k & bit
        }
    return held[0]


def sum_over_dp(terms):
    return jnp.sum(
        lax.all_to_all(terms.astype(BF), "dp", 0, 0, tiled=True).astype(F32), axis=0
    )


def local(
    text_embed,
    region_feats,
    box_coords,
    seg_ids,
    region_counts,
    send_index,
    recv_pos,
    w_proj,
    box_table,
    type_embed,
    pos_embed,
    gain_embed,
    bias_embed,
    w_qkv,
    w_mix,
    gain_mid,
    bias_mid,
    w_up,
    w_down,
    gain_final,
    bias_final,
    cotangent,
):
    parts = lax.axis_size("tensor")
    peers = lax.axis_size("dp")
    mine = lax.axis_index("tensor")
    row_count, text_len, width = text_embed.shape
    assert row_count == parts
    length = seg_ids.shape[1]
    slots = length - text_len
    stored = region_feats.shape[0]
    capacity = send_index.shape[2]
    bins = box_table.shape[1]
    group = w_qkv.shape[2]
    heads_here = group // HD
    chunk = width // parts
    share = width // peers

    def own(array):
        return lax.dynamic_index_in_dim(array, mine, 0, keepdims=False)

    def own_columns(array, k=0):
        return lax.dynamic_slice_in_dim(array, (mine ^ k) * chunk, chunk, array.ndim - 1)

    partial = reduce_shards(
        [
            jnp.dot(region_feats, own_columns(w_proj, k), preferred_element_type=F32)
            for k in range(parts)
        ]
    )
    corners = (
        (box_coords[:, :, None] == jnp.arange(bins, dtype=jnp.int32)[None, None, :])
        .astype(BF)
        .reshape(stored, -1)
    )
    boxed = jnp.dot(
        corners, own_columns(box_table).reshape(-1, chunk), preferred_element_type=F32
    )
    rows_low = (partial + boxed).astype(BF)
    send_flat = send_index.reshape(-1)
    send_pick = (send_flat[:, None] == jnp.arange(stored, dtype=jnp.int32)[None, :]).astype(BF)
    outgoing = jnp.dot(send_pick, rows_low, preferred_element_type=F32).astype(BF)
    incoming = lax.all_to_all(
        outgoing.reshape(peers, capacity, chunk), "dp", 0, 0, tiled=True
    ).reshape(peers * capacity, chunk)
    recv_flat = recv_pos.reshape(-1)
    recv_slot = jnp.where(
        recv_flat >= 0,
        (recv_flat // length) * slots + recv_flat % length - text_len,
        -1,
    )
    recv_pick = (
        jnp.arange(row_count * slots, dtype=jnp.int32)[:, None] == recv_slot[None, :]
    ).astype(BF)
    placed = jnp.dot(recv_pick, incoming, preferred_element_type=F32).astype(BF)
    placed = lax.all_to_all(placed.reshape(parts, slots, chunk), "tensor", 0, 0, tiled=True)
    placed = placed.transpose(1, 0, 2).reshape(slots, width)

    qkv_shards = gather_shards(w_qkv)
    mix_shards = gather_shards(w_mix)
    up_shards = gather_shards(w_up)
    down_shards = gather_shards(w_down)

    text_part = own(text_embed).astype(F32) + type_embed[0].astype(F32)
    region_part = placed.astype(F32) + type_embed[1].astype(F32)
    embedded = jnp.concatenate([text_part, region_part], axis=0) + pos_embed.astype(F32)
    hidden0, normed0, inverse0 = layer_norm(embedded, gain_embed, bias_embed)
    inputs0 = hidden0.astype(BF)
    allowed = key_mask(own(seg_ids), own(region_counts))
    heads, contexts, logsums = [], [], []
    attn = 0.0
    for k in range(parts):
        mixed = jnp.einsum("td,cde->cte", inputs0, qkv_shards[k], preferred_element_type=F32)
        mixed = mixed.astype(BF).reshape(3, length, heads_here, HD)
        context, logsum = attend(mixed[0], mixed[1], mixed[2], allowed)
        context = context.reshape(length, group)
        attn = attn + jnp.dot(context, mix_shards[k], preferred_element_type=F32)
        heads.append(mixed)
        contexts.append(context)
        logsums.append(logsum)
    hidden1, normed1, inverse1 = layer_norm(hidden0 + attn, gain_mid, bias_mid)
    inputs1 = hidden1.astype(BF)
    befores, actives = [], []
    ffn = 0.0
    for k in range(parts):
        before = jnp.dot(inputs1, up_shards[k], preferred_element_type=F32)
        active = jax.nn.gelu(before, approximate=False).astype(BF)
        ffn = ffn + jnp.dot(active, down_shards[k], preferred_element_type=F32)
        befores.append(before)
        actives.append(active)
    final, normed2, inverse2 = layer_norm(hidden1 + ffn, gain_final, bias_final)
    layer_output = lax.all_gather(final.astype(BF), "tensor", axis=0, tiled=False)

    grad_final = own(cotangent).astype(F32)
    grad_x2, grad_gain_final, grad_bias_final = norm_back(grad_final, normed2, inverse2, gain_final)
    grad_ffn = grad_x2.astype(BF)
    down_terms, up_terms = [], []
    back_one = 0.0
    for k in range(parts):
        down_terms.append(
            jnp.einsum("td,tf->df", grad_ffn, actives[k], preferred_element_type=F32)
        )
        grad_active = jnp.einsum("td,fd->tf", grad_ffn, down_shards[k], preferred_element_type=F32)
        slope = jax.vjp(lambda value: jax.nn.gelu(value, approximate=False), befores[k])[1]
        grad_before = slope(grad_active)[0].astype(BF)
        up_terms.append(
            jnp.einsum("td,tf->df", inputs1, grad_before, preferred_element_type=F32)
        )
        back_one = back_one + jnp.einsum(
            "tf,df->td", grad_before, up_shards[k], preferred_element_type=F32
        )
    sum_down = reduce_shards(down_terms)
    sum_up = reduce_shards(up_terms)
    grad_x1, grad_gain_mid, grad_bias_mid = norm_back(
        grad_x2 + back_one, normed1, inverse1, gain_mid
    )
    grad_attn = grad_x1.astype(BF)
    mix_terms, qkv_terms = [], []
    back_zero = 0.0
    for k in range(parts):
        mix_terms.append(
            jnp.einsum("td,te->de", grad_attn, contexts[k], preferred_element_type=F32)
        )
        grad_context = jnp.einsum(
            "td,ed->te", grad_attn, mix_shards[k], preferred_element_type=F32
        ).astype(BF)
        grad_mixed = jnp.stack(
            attend_back(
                heads[k][0],
                heads[k][1],
                heads[k][2],
                grad_context.reshape(length, heads_here, HD),
                logsums[k],
                allowed,
            )
        ).reshape(3, length, group)
        qkv_terms.append(
            jnp.einsum("td,cte->cde", inputs0, grad_mixed, preferred_element_type=F32)
        )
        back_zero = back_zero + jnp.einsum(
            "cte,cde->td", grad_mixed, qkv_shards[k], preferred_element_type=F32
        )
    sum_mix = reduce_shards(mix_terms)
    sum_qkv = reduce_shards(qkv_terms)
    grad_embedded, grad_gain_embed, grad_bias_embed = norm_back(
        grad_x1 + back_zero, normed0, inverse0, gain_embed
    )
    text_own = grad_embedded[:text_len]
    region_own = grad_embedded[text_len:]
    text_grad = lax.all_gather(text_own.astype(BF), "tensor", axis=0, tiled=False).astype(F32)

    vectors = jnp.stack(
        [
            jnp.sum(text_own, axis=0),
            jnp.sum(region_own, axis=0),
            grad_gain_embed,
            grad_bias_embed,
            grad_gain_mid,
            grad_bias_mid,
            grad_gain_final,
            grad_bias_final,
        ]
    )
    vector_count = vectors.shape[0]
    outward = jnp.concatenate([region_own, text_own, vectors], axis=0).astype(BF)
    outward = outward.reshape(-1, parts, chunk).transpose(1, 0, 2)
    inward = lax.all_to_all(outward, "tensor", 0, 0, tiled=True)
    returning = jnp.einsum(
        "js,jc->sc",
        recv_pick,
        inward[:, :slots].reshape(row_count * slots, chunk),
        preferred_element_type=F32,
    ).astype(BF)
    returned = lax.all_to_all(
        returning.reshape(peers, capacity, chunk), "dp", 0, 0, tiled=True
    ).reshape(peers * capacity, chunk)
    region_chunk = jnp.einsum(
        "sr,sc->rc", send_pick, returned, preferred_element_type=F32
    ).astype(BF)
    grad_regions = lax.all_gather(region_chunk, "tensor", axis=1, tiled=True)
    proj_term = jnp.einsum("sd,sf->df", grad_regions, region_feats, preferred_element_type=F32)
    feat_grad = jnp.einsum("sd,fd->sf", grad_regions, w_proj, preferred_element_type=F32)
    box_term = jnp.einsum("sb,sc->bc", corners, region_chunk, preferred_element_type=F32)

    summed = jnp.sum(inward.astype(F32), axis=0)
    pos_term = jnp.concatenate([summed[slots:length], summed[:slots]], axis=0)
    bin_share = bins // peers
    pos_share = length // peers
    bundle = jnp.concatenate(
        [
            pos_term.reshape(peers, pos_share, chunk),
            box_term.reshape(-1, peers, bin_share, chunk)
            .transpose(1, 0, 2, 3)
            .reshape(peers, -1, chunk),
            jnp.broadcast_to(summed[length:], (peers, vector_count, chunk)),
        ],
        axis=1,
    )
    bundle = lax.all_gather(sum_over_dp(bundle), "tensor", axis=1, tiled=True)
    grad_pos = bundle[:pos_share]
    grad_box = bundle[pos_share:-vector_count].reshape(-1, bin_share, width)
    vectors = lax.dynamic_slice_in_dim(
        bundle[-vector_count:], lax.axis_index("dp") * share, share, 1
    )

    grad_down = sum_over_dp(sum_down.reshape(peers, share, -1)).T
    grad_up = sum_over_dp(sum_up.reshape(peers, share, -1))
    grad_mix = sum_over_dp(sum_mix.reshape(peers, share, -1)).T
    grad_qkv = sum_over_dp(sum_qkv.reshape(3, peers, share, group).transpose(1, 0, 2, 3))
    grad_proj = sum_over_dp(proj_term.reshape(peers, share, -1)).T
    return (
        layer_output,
        text_grad,
        feat_grad,
        grad_proj,
        grad_box,
        vectors[:2],
        grad_pos,
        vectors[2],
        vectors[3],
        grad_qkv,
        grad_mix,
        vectors[4],
        vectors[5],
        grad_up,
        grad_down,
        vectors[6],
        vectors[7],
    )


def solution(mesh):
    return jax.shard_map(
        local,
        mesh=mesh,
        in_specs=(
            P("dp", None, None),
            P("dp", "tensor"),
            P("dp", None),
            P("dp", None),
            P("dp"),
            P("dp", None, None),
            P("dp", None, None),
            P("tensor", None),
            P(),
            P(),
            P(),
            P(),
            P(),
            P(None, None, "tensor"),
            P("tensor", None),
            P(),
            P(),
            P(None, "tensor"),
            P("tensor", None),
            P(),
            P(),
            P("dp", None, None),
        ),
        out_specs=(
            P("dp", None, None),
            P("dp", None, None),
            P("dp", "tensor"),
            P("tensor", "dp"),
            P(None, "dp", None),
            P(None, "dp"),
            P("dp", None),
            P("dp"),
            P("dp"),
            P(None, "dp", "tensor"),
            P("tensor", "dp"),
            P("dp"),
            P("dp"),
            P("dp", "tensor"),
            P("tensor", "dp"),
            P("dp"),
            P("dp"),
        ),
        check_vma=False,
    )
```

```python
import jax
import jax.numpy as jnp
from jax import lax
from jax.experimental import pallas as pl
from jax.experimental.pallas import tpu as pltpu
from jax.sharding import PartitionSpec as P

HD = 64
LT = 384
EPSILON = 1e-06
NEGATIVE = -1000000000.0
BF = jnp.bfloat16
F32 = jnp.float32


def layer_norm(values, gain, bias):
    mean = jnp.mean(values, axis=-1, keepdims=True)
    centred = values - mean
    variance = jnp.mean(centred * centred, axis=-1, keepdims=True)
    inverse = lax.rsqrt(variance + EPSILON)
    normed = centred * inverse
    return (normed * gain + bias, normed, inverse)


def key_mask(seg_row, count):
    length = seg_row.shape[0]
    places = jnp.arange(length, dtype=jnp.int32)
    usable = places < LT + count
    same = seg_row[:, None] == seg_row[None, :]
    return same & (usable[None, :] | (places[:, None] == places[None, :]))


VMEM_BYTES = 52 << 20
ROOT_HALF = 0.7071067811865476
DENSITY = 0.3989422804014327


def dot(a, b):
    return jnp.dot(a, b, preferred_element_type=F32)


def dot_nt(a, b):
    return lax.dot_general(a, b, (((1,), (1,)), ((), ())), preferred_element_type=F32)


def dot_tn(a, b):
    return lax.dot_general(a, b, (((0,), (0,)), ((), ())), preferred_element_type=F32)


def any_specs(count):
    return [pl.BlockSpec(memory_space=pl.ANY)] * count


def smem_spec():
    return [pl.BlockSpec(memory_space=pltpu.SMEM)]


def vmem_specs(count):
    return [pl.BlockSpec(memory_space=pltpu.VMEM)] * count


def call(body, outs, in_specs, out_specs, scratch, flops):
    return pl.pallas_call(
        body,
        out_shape=[jax.ShapeDtypeStruct(shape, kind) for shape, kind in outs],
        in_specs=in_specs,
        out_specs=out_specs,
        scratch_shapes=scratch,
        compiler_params=pltpu.CompilerParams(vmem_limit_bytes=VMEM_BYTES),
        cost_estimate=pl.CostEstimate(flops=flops, bytes_accessed=16 << 20, transcendentals=0),
    )


def attend_kernel(heads, sizes, side_ref, x_ref, z_ref, allow_ref, *rest):
    count = len(sizes)
    shards, rest = regroup(rest, sizes)
    zout_ref, helds, lses = rest[0], rest[1 : 1 + count], rest[1 + count : 1 + 2 * count]
    weights, sems = rest[1 + 2 * count :]
    started, _ = fetch_shards(shards, weights, side_ref[0], sems)
    length, width = x_ref.shape
    group = heads * HD
    block = 128
    lane = lax.broadcasted_iota(jnp.int32, (block, 128), 1)
    for i in range(count):
        for copy in started[i]:
            copy.wait()
        w_ref, held, lse_ref = weights.at[i], helds[i], lses[i]
        mixed = dot(x_ref[...], w_ref[...])
        held[:, group : 2 * group] = (mixed[:, group : 2 * group] * HD ** (-0.5)).astype(BF)
        held[:, 2 * group :] = mixed[:, 2 * group :].astype(BF)

        def rows(b, carry):
            at = pl.ds(pl.multiple_of(b * block, block), block)
            columns = jnp.zeros((block, 128), F32)
            allow = allow_ref[at, :] > 0.5
            for h in range(heads):
                q = held[at, group + h * HD : group + (h + 1) * HD]
                k = held[:, 2 * group + h * HD : 2 * group + (h + 1) * HD]
                v = held[:, 3 * group + h * HD : 3 * group + (h + 1) * HD]
                scores = jnp.where(allow, dot_nt(q, k), NEGATIVE)
                top = jnp.max(scores, axis=1, keepdims=True)
                raised = jnp.exp(scores - top)
                total = jnp.sum(raised, axis=1, keepdims=True)
                context = dot(raised.astype(BF), v) / total
                held[at, h * HD : (h + 1) * HD] = context.astype(BF)
                columns = jnp.where(lane == h, top + jnp.log(total), columns)
            lse_ref[:, at] = columns.T[:8, :]
            return carry

        lax.fori_loop(0, length // block, rows, 0)
        if i == 0:
            zout_ref[...] = z_ref[...] + dot_nt(held[:, :group], w_ref[:, :group])
        else:
            zout_ref[...] += dot_nt(held[:, :group], w_ref[:, :group])


def attend_call(heads, side, x, z, allow, shards):
    length, width = x.shape
    n = len(shards)
    sizes = [len(pieces) for pieces in shards]
    outs = [((length, width), F32)] + [((length, width), BF)] * n + [((8, length), F32)] * n
    got = call(
        lambda *refs: attend_kernel(heads, sizes, *refs),
        outs,
        smem_spec() + vmem_specs(3) + any_specs(sum(sizes)),
        vmem_specs(len(outs)),
        [pltpu.VMEM((n, width, width), BF), pltpu.SemaphoreType.DMA((sum(sizes),))],
        n * 2_000_000_000,
    )(side, x, z, allow, *sum(shards, []))
    return got[0], got[1 : 1 + n], got[1 + n :]


def attend_back_kernel(heads, sizes, side_ref, g_ref, gt_ref, xt_ref, acc_ref, allow_ref, *rest):
    count = len(sizes)
    shards, rest = regroup(rest, sizes)
    helds, lses = rest[:count], rest[count : 2 * count]
    accout_ref, terms = rest[2 * count], rest[2 * count + 1 : 3 * count + 1]
    gc_ref, grads, dq_ref, delta_ref, weights, sems = rest[3 * count + 1 :]
    started, _ = fetch_shards(shards, weights, side_ref[0], sems)
    length, width = g_ref.shape
    group = heads * HD
    block = 128
    lane = lax.broadcasted_iota(jnp.int32, (length, 128), 1)
    for i in range(count):
        for copy in started[i]:
            copy.wait()
        w_ref, held, lse_ref = weights.at[i], helds[i], lses[i]
        low = dot(g_ref[...], w_ref[:, :group]).astype(BF)
        gc_ref[...] = low
        product = low.astype(F32) * held[:, :group].astype(F32)
        columns = jnp.zeros((length, 128), F32)
        for h in range(heads):
            inner = jnp.sum(product[:, h * HD : (h + 1) * HD], axis=1, keepdims=True)
            columns = jnp.where(lane == h, inner, columns)
        delta_ref[...] = columns.T[:8, :]
        dq_ref[...] = jnp.zeros_like(dq_ref)
        grads[:, :group] = jnp.zeros((length, group), BF)

        def rows(b, carry):
            at = pl.ds(pl.multiple_of(b * block, block), block)
            allow = allow_ref[at, :] > 0.5
            for h in range(heads):
                q = held[:, group + h * HD : group + (h + 1) * HD]
                k = held[at, 2 * group + h * HD : 2 * group + (h + 1) * HD]
                v = held[at, 3 * group + h * HD : 3 * group + (h + 1) * HD]
                gc = gc_ref[:, h * HD : (h + 1) * HD]
                scores = jnp.where(allow, dot_nt(k, q), NEGATIVE)
                probs = jnp.exp(scores - lse_ref[h : h + 1, :])
                grad_probs = dot_nt(v, gc)
                grad_scores = (probs * (grad_probs - delta_ref[h : h + 1, :])).astype(BF)
                grads[at, 3 * group + h * HD : 3 * group + (h + 1) * HD] = dot(
                    probs.astype(BF), gc
                ).astype(BF)
                grads[at, 2 * group + h * HD : 2 * group + (h + 1) * HD] = dot(
                    grad_scores, q
                ).astype(BF)
                dq_ref[h * HD : (h + 1) * HD, :] += dot_tn(k, grad_scores)
            return carry

        lax.fori_loop(0, length // block, rows, 0)
        grads[:, group : 2 * group] = (dq_ref[...] * HD ** (-0.5)).T.astype(BF)
        if i == 0:
            accout_ref[...] = acc_ref[...] + dot_nt(grads[...], w_ref[...])
        else:
            accout_ref[...] += dot_nt(grads[...], w_ref[...])
        terms[i][...] = dot(xt_ref[...], grads[...]).astype(BF)
        terms[i][:, :group] = dot(gt_ref[...], held[:, :group]).astype(BF)


def attend_back_call(heads, side, g, gt, xt, acc, allow, shards, helds, lses):
    length, width = g.shape
    n = len(shards)
    sizes = [len(pieces) for pieces in shards]
    group = heads * HD
    outs = [((length, width), F32)] + [((width, width), BF)] * n
    got = call(
        lambda *refs: attend_back_kernel(heads, sizes, *refs),
        outs,
        smem_spec() + vmem_specs(5) + any_specs(sum(sizes)) + vmem_specs(2 * n),
        vmem_specs(len(outs)),
        [
            pltpu.VMEM((length, group), BF),
            pltpu.VMEM((length, width), BF),
            pltpu.VMEM((group, length), F32),
            pltpu.VMEM((8, length), F32),
            pltpu.VMEM((n, width, width), BF),
            pltpu.SemaphoreType.DMA((sum(sizes),)),
        ],
        n * 4_000_000_000,
    )(side, g, gt, xt, acc, allow, *sum(shards, []), *helds, *lses)
    return got[0], got[1:]


def erf(x):
    x = jnp.clip(x, -4.0, 4.0)
    s = x * x
    top = jnp.full_like(x, -2.72614225801306e-10)
    for c in (
        2.77068142495902e-08,
        -2.10102402082508e-06,
        -5.69250639462346e-05,
        -7.34990630326855e-04,
        -2.95459980854025e-03,
        -1.60960333262415e-02,
    ):
        top = top * s + c
    base = jnp.full_like(x, -1.45660718464996e-05)
    for c in (
        -2.13374055278905e-04,
        -1.68282697438203e-03,
        -7.37332916720468e-03,
        -1.42647390514189e-02,
    ):
        base = base * s + c
    return x * top / base


def norm_back(grad, values, gain):
    _, normed, inverse = layer_norm(values, gain, 0.0)
    scaled = grad * gain
    mean_grad = jnp.mean(scaled, axis=-1, keepdims=True)
    mean_proj = jnp.mean(scaled * normed, axis=-1, keepdims=True)
    return (
        inverse * (scaled - mean_grad - normed * mean_proj),
        jnp.sum(grad * normed, axis=0, keepdims=True),
        jnp.sum(grad, axis=0, keepdims=True),
    )


def regroup(flat, sizes):
    flat = list(flat)
    return [[flat.pop(0) for _ in range(size)] for size in sizes], flat


def fetch_shards(shards, target, side, sems, base=0):
    started = []
    for i, pieces in enumerate(shards):
        copies = []
        for j, piece in enumerate(pieces):
            rows = piece.shape[0]
            at = pl.ds(pl.multiple_of((side if j == 0 else 1 - side) * rows, 16), rows)
            place = target.at[i] if len(pieces) == 1 else target.at[i, at]
            copies.append(pltpu.make_async_copy(piece, place, sems.at[base]))
            copies[-1].start()
            base += 1
        started.append(copies)
    return started, base


def forward_kernel(
    parts, sizes, side_ref, z_ref, cot_ref, gm_ref, bm_ref, gf_ref, bf_ref, *rest
):
    up_shards, rest = regroup(rest, sizes)
    down_shards, rest = regroup(rest, sizes)
    slope_ref, terms = rest[0], rest[1 : parts + 1]
    out_ref, x1t_ref, gx2_ref, g_ref, vec_ref = rest[parts + 1 : parts + 6]
    ups, downs, actives, ffn_ref, x1_ref, gt_ref, sems = rest[parts + 6 :]
    up_started, base = fetch_shards(up_shards, ups, side_ref[1], sems)
    down_started, _ = fetch_shards(down_shards, downs, side_ref[2], sems, base)
    length, width = z_ref.shape
    block = 256
    vec_ref[...] = jnp.zeros_like(vec_ref)
    for b in range(length // block):
        at = slice(b * block, (b + 1) * block)
        hidden1, _, _ = layer_norm(z_ref[at, :], gm_ref[...], bm_ref[...])
        x1_ref[at, :] = hidden1.astype(BF)
        ffn_ref[at, :] = hidden1
        for k in range(parts):
            if b == 0:
                for copy in up_started[k]:
                    copy.wait()
            before = dot(x1_ref[at, :], ups[k])
            half = 0.5 + 0.5 * erf(before * ROOT_HALF)
            slope_ref[k, at, :] = (
                half + before * (DENSITY * jnp.exp(-0.5 * before * before))
            ).astype(BF)
            actives[k, at, :] = (before * half).astype(BF)
            if b == 0:
                for copy in down_started[k]:
                    copy.wait()
            ffn_ref[at, :] += dot(actives[k, at, :], downs[k])
        final, normed, inverse = layer_norm(ffn_ref[at, :], gf_ref[...], bf_ref[...])
        out_ref[at, :] = final.astype(BF)
        grad_in, gain_sum, bias_sum = norm_back(
            cot_ref[at, :].astype(F32), ffn_ref[at, :], gf_ref[...]
        )
        vec_ref[0:1, :] += gain_sum
        vec_ref[1:2, :] += bias_sum
        gx2_ref[at, :] = grad_in
        g_ref[at, :] = grad_in.astype(BF)
    gt_ref[...] = g_ref[...].T
    for k in range(parts):
        terms[k][...] = dot(gt_ref[...], actives[k]).astype(BF)
    x1t_ref[...] = x1_ref[...].T


def forward_call(side, z, cot, gm, bm, gf, bf, up, down):
    length, width = z.shape
    n = len(up)
    sizes = [len(pieces) for pieces in up]
    inner = up[0][0].shape[1]
    outs = (
        [((n, length, inner), BF)]
        + [((width, inner), BF)] * n
        + [
            ((length, width), BF),
            ((width, length), BF),
            ((length, width), F32),
            ((length, width), BF),
            ((8, width), F32),
        ]
    )
    got = call(
        lambda *refs: forward_kernel(n, sizes, *refs),
        outs,
        smem_spec() + vmem_specs(6) + any_specs(2 * sum(sizes)),
        vmem_specs(len(outs)),
        [
            pltpu.VMEM((n, width, inner), BF),
            pltpu.VMEM((n, inner, width), BF),
            pltpu.VMEM((n, length, inner), BF),
            pltpu.VMEM((length, width), F32),
            pltpu.VMEM((length, width), BF),
            pltpu.VMEM((width, length), BF),
            pltpu.SemaphoreType.DMA((2 * sum(sizes),)),
        ],
        8_000_000_000,
    )(side, z, cot, gm, bm, gf, bf, *sum(up, []), *sum(down, []))
    return got[0], got[1 : n + 1], got[n + 1 :]


def backward_kernel(
    parts, sizes, side_ref, z_ref, gx2_ref, g_ref, x1t_ref, gm_ref, *rest
):
    up_shards, rest = regroup(rest, sizes)
    down_shards, rest = regroup(rest, sizes)
    slope_any, *rest = rest
    terms = rest[:parts]
    gx1_ref, ga_ref, gat_ref, vec_ref, gb_ref, ups, downs, slopes, sems = rest[parts:]
    down_started, base = fetch_shards(down_shards, downs, side_ref[2], sems)
    up_started, base = fetch_shards(up_shards, ups, side_ref[1], sems, base)
    slope_copies = []
    for k in range(parts):
        slope_copies.append(
            pltpu.make_async_copy(slope_any.at[k], slopes.at[k], sems.at[base + k])
        )
        slope_copies[k].start()
    gx1_ref[...] = gx2_ref[...]
    for k in sorted(range(parts), key=lambda k: (1 - k % 2, k)):
        for copy in (*down_started[k], slope_copies[k], *up_started[k]):
            copy.wait()
        gb_ref[...] = (dot_nt(g_ref[...], downs[k]) * slopes[k].astype(F32)).astype(BF)
        terms[k][...] = dot(x1t_ref[...], gb_ref[...]).astype(BF)
        gx1_ref[...] += dot_nt(gb_ref[...], ups[k])
    grad_in, gain_sum, bias_sum = norm_back(gx1_ref[...], z_ref[...], gm_ref[...])
    vec_ref[...] = jnp.zeros_like(vec_ref)
    vec_ref[0:1, :] = gain_sum
    vec_ref[1:2, :] = bias_sum
    gx1_ref[...] = grad_in
    ga_ref[...] = grad_in.astype(BF)
    gat_ref[...] = ga_ref[...].T


def backward_call(side, z, gx2, g, x1t, gm, up, down, slope):
    length, width = z.shape
    n = len(up)
    sizes = [len(pieces) for pieces in up]
    inner = up[0][0].shape[1]
    outs = [((width, inner), BF)] * n + [
        ((length, width), F32),
        ((length, width), BF),
        ((width, length), BF),
        ((8, width), F32),
    ]
    got = call(
        lambda *refs: backward_kernel(n, sizes, *refs),
        outs,
        smem_spec() + vmem_specs(5) + any_specs(2 * sum(sizes) + 1),
        vmem_specs(len(outs)),
        [
            pltpu.VMEM((length, inner), BF),
            pltpu.VMEM((n, width, inner), BF),
            pltpu.VMEM((n, inner, width), BF),
            pltpu.VMEM((n, length, inner), BF),
            pltpu.SemaphoreType.DMA((2 * sum(sizes) + n,)),
        ],
        8_000_000_000,
    )(side, z, gx2, g, x1t, gm, *sum(up, []), *sum(down, []), slope)
    return got[:n], got[n:]


def pack_kernel(mix_ref, qkv_ref, out_ref):
    group = mix_ref.shape[0]
    out_ref[:, :group] = mix_ref[...].T
    for c in range(qkv_ref.shape[0]):
        out_ref[:, (c + 1) * group : (c + 2) * group] = qkv_ref[c]


def choose(index, count, step, source, store):
    for c in range(count):

        @pl.when(index == c)
        def _(c=c):
            store(source[:, c * step : (c + 1) * step])


def project_kernel(parts, mine_ref, feats_ref, w_ref, *rest):
    outs, full = rest[:parts], rest[parts]
    full[...] = dot(feats_ref[...], w_ref[...])
    step = outs[0].shape[1]
    for k, out in enumerate(outs):

        def store(value, out=out):
            out[...] = value.astype(out.dtype)

        choose(mine_ref[0] ^ k, parts, step, full, store)


def outgoing_kernel(parts, mine_ref, own_ref, near_ref, far_ref, box_ref, table_ref, pick_ref, out_ref, full, low):
    stored, chunk = own_ref.shape
    bins = table_ref.shape[1]
    places = lax.broadcasted_iota(jnp.int32, (stored, bins), 1)
    full[...] = jnp.zeros_like(full)
    for c in range(table_ref.shape[0]):
        full[...] += dot((box_ref[:, c : c + 1] == places).astype(BF), table_ref[c])

    def store(value):
        total = own_ref[...] + near_ref[...].astype(F32) + far_ref[...].astype(F32)
        low[...] = (total + value).astype(BF)

    choose(mine_ref[0], parts, chunk, full, store)
    slots = out_ref.shape[0]
    regions = lax.broadcasted_iota(jnp.int32, (slots, stored), 1)
    out_ref[...] = dot((pick_ref[...] == regions).astype(BF), low[...]).astype(BF)


def move_rows_kernel(pick_ref, rows_ref, out_ref):
    shape = (out_ref.shape[0], rows_ref.shape[0])
    places = lax.broadcasted_iota(jnp.int32, shape, 0)
    out_ref[...] = dot((pick_ref[...] == places).astype(BF), rows_ref[...]).astype(BF)


def take_rows_kernel(pick_ref, rows_ref, out_ref):
    shape = (out_ref.shape[0], rows_ref.shape[0])
    places = lax.broadcasted_iota(jnp.int32, shape, 1)
    out_ref[...] = dot((pick_ref[...] == places).astype(BF), rows_ref[...]).astype(BF)


def embed_kernel(parts, text_ref, placed_ref, type_ref, pos_ref, gain_ref, bias_ref, emb_ref, hid_ref, x_ref, xt_ref):
    text_len = text_ref.shape[0]
    chunk = placed_ref.shape[2]
    types = type_ref[...].astype(F32)
    pos = pos_ref[...].astype(F32)
    emb_ref[:text_len, :] = text_ref[...].astype(F32) + types[0:1, :] + pos[:text_len, :]
    for c in range(parts):
        at = slice(c * chunk, (c + 1) * chunk)
        emb_ref[text_len:, at] = placed_ref[c].astype(F32)
    emb_ref[text_len:, :] += types[1:2, :] + pos[text_len:, :]
    hidden, _, _ = layer_norm(emb_ref[...], gain_ref[...], bias_ref[...])
    hid_ref[...] = hidden
    x_ref[...] = hidden.astype(BF)
    xt_ref[...] = x_ref[...].T


def embed_back_kernel(parts, grad_ref, emb_ref, gain_ref, mid_ref, fin_ref, text_ref, reg_ref, rest_ref, vec):
    text_len = text_ref.shape[0]
    chunk = reg_ref.shape[2]
    grad_in, gain_sum, bias_sum = norm_back(grad_ref[...], emb_ref[...], gain_ref[...])
    low = grad_in.astype(BF)
    text_ref[...] = low[:text_len, :]
    vec[...] = jnp.zeros_like(vec)
    vec[0:1, :] = jnp.sum(grad_in[:text_len, :], axis=0, keepdims=True)
    vec[1:2, :] = jnp.sum(grad_in[text_len:, :], axis=0, keepdims=True)
    vec[2:3, :] = gain_sum
    vec[3:4, :] = bias_sum
    vec[4:6, :] = mid_ref[0:2, :]
    vec[6:8, :] = fin_ref[0:2, :]
    vectors = vec[...].astype(BF)
    for c in range(parts):
        at = slice(c * chunk, (c + 1) * chunk)
        reg_ref[c] = low[text_len:, at]
        rest_ref[c, :text_len, :] = low[:text_len, at]
        rest_ref[c, text_len:, :] = vectors[:, at]


def box_kernel(pick_ref, rows_ref, box_ref, chunk_ref, term_ref):
    move_rows_kernel(pick_ref, rows_ref, chunk_ref)
    bins = term_ref.shape[1]
    places = lax.broadcasted_iota(jnp.int32, (bins, chunk_ref.shape[0]), 0)
    for c in range(term_ref.shape[0]):
        term_ref[c] = dot((box_ref[c : c + 1, :] == places).astype(BF), chunk_ref[...])


def project_back_kernel(parts, chunks_ref, feats_ref, w_ref, grad_ref, term_ref, full):
    chunk = chunks_ref.shape[2]
    for c in range(parts):
        full[:, c * chunk : (c + 1) * chunk] = chunks_ref[c]
    grad_ref[...] = dot_nt(full[...], w_ref[...])
    term_ref[...] = dot(full[...].T, feats_ref[...]).astype(BF)


def spread_kernel(parts, chunks_ref, out_ref):
    chunk = chunks_ref.shape[2]
    for c in range(parts):
        out_ref[:, c * chunk : (c + 1) * chunk] = chunks_ref[c]


def small_call(body, args, outs, scratch=(), scalar=False, flops=500_000_000):
    specs = vmem_specs(len(args))
    if scalar:
        specs[0] = pl.BlockSpec(memory_space=pltpu.SMEM)
    got = call(body, outs, specs, vmem_specs(len(outs)), list(scratch), flops)(*args)
    return got[0] if len(outs) == 1 else got


def swap(value, axis, bit):
    count = lax.axis_size(axis)
    return lax.ppermute(value, axis, [(i, i ^ bit) for i in range(count)])


def bits_of(axis):
    count = lax.axis_size(axis)
    return [1 << i for i in range(count.bit_length() - 1)]


def tie(first, second):
    return lax.optimization_barrier((first, second))


def far_half(shard, bit):
    rows = shard.shape[0] // 2
    side = (lax.axis_index("dp") // bit) % 2
    return swap(lax.dynamic_slice_in_dim(shard, side * rows, rows, 0), "tensor", 2)


def gather_shards(shard, half, other):
    return [
        [shard],
        [swap(shard, "tensor", 1)],
        [half, other],
        [swap(half, "tensor", 1), swap(other, "tensor", 1)],
    ]


def fold(held, bit):
    moved = {
        k: swap(total(v).astype(BF), "tensor", bit) for k, v in held.items() if k & bit
    }
    return {k: v + [moved[k | bit]] for k, v in held.items() if not k & bit}


def total(summands):
    return sum(value.astype(F32) for value in summands)


def terms_of(terms):
    return {k: [term] for k, term in enumerate(terms)}


def sum_over_dp(term):
    bits = bits_of("dp")
    me = lax.axis_index("dp")
    rows, columns = term.shape
    held = term.reshape([2] * len(bits) + [rows >> len(bits), columns])
    for step, bit in enumerate(bits):
        axis = len(bits) - 1 - step
        side = (me // bit) % 2
        sent = lax.dynamic_index_in_dim(held, 1 - side, axis, keepdims=False)
        kept = lax.dynamic_index_in_dim(held, side, axis, keepdims=False)
        held = kept.astype(F32) + swap(sent.astype(BF), "dp", bit).astype(F32)
    return held


def local(
    text_embed,
    region_feats,
    box_coords,
    seg_ids,
    region_counts,
    send_index,
    recv_pos,
    w_proj,
    box_table,
    type_embed,
    pos_embed,
    gain_embed,
    bias_embed,
    w_qkv,
    w_mix,
    gain_mid,
    bias_mid,
    w_up,
    w_down,
    gain_final,
    bias_final,
    cotangent,
):
    parts = lax.axis_size("tensor")
    peers = lax.axis_size("dp")
    mine = lax.axis_index("tensor")
    mine_now = mine.reshape(1).astype(jnp.int32)
    dp_now = lax.axis_index("dp")
    sides = jnp.stack([dp_now % 2, dp_now % 2, (dp_now // 2) % 2]).astype(jnp.int32)
    row_count, text_len, width = text_embed.shape
    assert row_count == parts == 4
    length = seg_ids.shape[1]
    slots = length - text_len
    stored, depth = region_feats.shape
    capacity = send_index.shape[2]
    bins = box_table.shape[1]
    group = w_qkv.shape[2]
    heads = group // HD
    chunk = width // parts
    share = width // peers
    wire = peers * capacity

    def own(array):
        return lax.dynamic_index_in_dim(array, mine, 0, keepdims=False)

    def line(vector):
        return vector.reshape(1, width)

    held = small_call(
        lambda *refs: project_kernel(parts, *refs),
        [mine_now, region_feats, w_proj],
        [((stored, chunk), F32 if k == 0 else BF) for k in range(parts)],
        [pltpu.VMEM((stored, width), F32)],
        scalar=True,
    )
    near = swap(held[1], "tensor", 1)
    across = (held[2].astype(F32) + swap(held[3], "tensor", 1).astype(F32)).astype(BF)

    across, (w_mix, w_qkv) = tie(across, (w_mix, w_qkv))
    far = swap(across, "tensor", 2)
    packed = small_call(pack_kernel, [w_mix, w_qkv], [((width, width), BF)])
    far, packed = tie(far, packed)
    att_half = far_half(packed, 1)

    send_flat = send_index.reshape(-1)
    recv_flat = recv_pos.reshape(-1)
    recv_slot = jnp.where(
        recv_flat >= 0,
        (recv_flat // length) * slots + recv_flat % length - text_len,
        -1,
    )
    send_line, send_column = send_flat.reshape(1, wire), send_flat.reshape(wire, 1)
    recv_line, recv_column = recv_slot.reshape(1, wire), recv_slot.reshape(wire, 1)
    outgoing = small_call(
        lambda *refs: outgoing_kernel(parts, *refs),
        [mine_now, held[0], near, far, box_coords, box_table, send_column],
        [((wire, chunk), BF)],
        [pltpu.VMEM((stored, width), F32), pltpu.VMEM((stored, chunk), BF)],
        scalar=True,
    )
    outgoing, w_up = tie(outgoing, w_up)
    up_half = far_half(w_up, 1)
    incoming = lax.all_to_all(
        outgoing.reshape(peers, capacity, chunk), "dp", 0, 0, tiled=True
    ).reshape(wire, chunk)
    incoming, att_half = tie(incoming, att_half)
    att_other = swap(att_half, "dp", 1)
    placed = small_call(
        move_rows_kernel, [recv_line, incoming], [((row_count * slots, chunk), BF)]
    )
    placed = lax.all_to_all(placed.reshape(parts, slots, chunk), "tensor", 0, 0, tiled=True)
    placed, w_down = tie(placed, w_down)
    down_half = far_half(w_down, 2)

    embedded, hidden0, inputs0, inputs0_turned = small_call(
        lambda *refs: embed_kernel(parts, *refs),
        [own(text_embed), placed, type_embed, pos_embed, line(gain_embed), line(bias_embed)],
        [
            ((length, width), F32),
            ((length, width), F32),
            ((length, width), BF),
            ((width, length), BF),
        ],
    )
    allowed = key_mask(own(seg_ids), own(region_counts))
    allow = allowed.astype(F32)
    allow_turned = allowed.T.astype(F32)

    (hidden0, inputs0), (up_half, att_other) = tie((hidden0, inputs0), (up_half, att_other))
    up_other = swap(up_half, "dp", 1)
    att_shards = gather_shards(packed, att_half, att_other)
    z, near_helds, near_lses = attend_call(heads, sides, inputs0, hidden0, allow, att_shards[:2])
    z, (up_other, down_half) = tie(z, (up_other, down_half))
    down_other = swap(down_half, "dp", 2)
    up = gather_shards(w_up, up_half, up_other)
    z, far_helds, far_lses = attend_call(heads, sides, inputs0, z, allow, att_shards[2:])
    helds, lses = near_helds + far_helds, near_lses + far_lses
    z, down_other = tie(z, down_other)
    down = gather_shards(w_down, down_half, down_other)
    slopes, down_terms, (final, x1t, grad_x2, grad_ffn, final_vectors) = forward_call(
        sides,
        z,
        own(cotangent),
        line(gain_mid),
        line(bias_mid),
        line(gain_final),
        line(bias_final),
        up,
        down,
    )
    layer_output = lax.all_gather(final, "tensor", axis=0, tiled=False)
    sum_down = fold(terms_of(down_terms), 1)

    up_terms, (grad_x1, grad_attn, grad_attn_turned, mid_vectors) = backward_call(
        sides, z, grad_x2, grad_ffn, x1t, line(gain_mid), up, down, slopes
    )
    (grad_attn, grad_x1), sum_down = tie((grad_attn, grad_x1), sum_down)
    sum_down = fold(sum_down, 2)[0]
    sum_up = fold(terms_of(up_terms), 1)
    total0 = grad_x1
    att_terms = [None] * parts
    for at in (1, 0):
        picked = range(at, parts, 2)
        total0, terms = attend_back_call(
            heads,
            sides,
            grad_attn,
            grad_attn_turned,
            inputs0_turned,
            total0,
            allow_turned,
            [att_shards[k] for k in picked],
            [helds[k] for k in picked],
            [lses[k] for k in picked],
        )
        for k, term in zip(picked, terms, strict=True):
            att_terms[k] = term
        if at:
            total0, sum_up = tie(total0, sum_up)
            sum_up = fold(sum_up, 2)[0]
    total0, sum_down = tie(total0, sum_down)
    sum_att = fold(terms_of(att_terms), 1)

    text_own, regions_out, rest_out = small_call(
        lambda *refs: embed_back_kernel(parts, *refs),
        [total0, embedded, line(gain_embed), mid_vectors, final_vectors],
        [
            ((text_len, width), BF),
            ((parts, slots, chunk), BF),
            ((parts, text_len + 16, chunk), BF),
        ],
        [pltpu.VMEM((16, width), F32)],
    )
    regions_in = lax.all_to_all(regions_out, "tensor", 0, 0, tiled=True)
    regions_in, sum_att = tie(regions_in, sum_att)
    sum_att = fold(sum_att, 2)[0]
    returning = small_call(
        take_rows_kernel,
        [recv_column, regions_in.reshape(row_count * slots, chunk)],
        [((wire, chunk), BF)],
    )
    returned = lax.all_to_all(
        returning.reshape(peers, capacity, chunk), "dp", 0, 0, tiled=True
    ).reshape(wire, chunk)
    region_chunk, box_term = small_call(
        box_kernel,
        [send_line, returned, box_coords.T],
        [((stored, chunk), BF), ((box_table.shape[0], bins, chunk), F32)],
    )
    region_chunks = lax.all_gather(region_chunk, "tensor", axis=0, tiled=False)
    feat_grad, proj_term = small_call(
        lambda *refs: project_back_kernel(parts, *refs),
        [region_chunks, region_feats, w_proj],
        [((stored, depth), F32), ((width, depth), BF)],
        [pltpu.VMEM((stored, width), BF)],
    )

    rest_in = lax.all_to_all(rest_out, "tensor", 0, 0, tiled=True)
    text_grad = lax.all_gather(text_own, "tensor", axis=0, tiled=False).astype(F32)
    summed = jnp.sum(rest_in.astype(F32), axis=0)
    pos_term = jnp.concatenate(
        [summed[:text_len], jnp.sum(regions_in.astype(F32), axis=0)], axis=0
    )
    bin_share = bins // peers
    pos_share = length // peers
    bundle = jnp.concatenate(
        [
            pos_term.reshape(peers, pos_share, chunk),
            box_term.reshape(-1, peers, bin_share, chunk)
            .transpose(1, 0, 2, 3)
            .reshape(peers, -1, chunk),
            jnp.broadcast_to(summed[text_len:], (peers, 16, chunk)),
        ],
        axis=1,
    ).astype(BF)
    bundle = jnp.sum(
        lax.all_to_all(bundle, "dp", 0, 0, tiled=True).astype(F32), axis=0
    )
    bundle = lax.all_gather(bundle, "tensor", axis=0, tiled=False)
    bundle = small_call(
        lambda *refs: spread_kernel(parts, *refs), [bundle], [((bundle.shape[1], width), F32)]
    )
    grad_pos = bundle[:pos_share]
    grad_box = bundle[pos_share:-16].reshape(-1, bin_share, width)
    vectors = lax.dynamic_slice_in_dim(bundle[-16:], lax.axis_index("dp") * share, share, 1)

    grad_down = sum_over_dp(total(sum_down)).T
    grad_up = sum_over_dp(total(sum_up))
    grad_att = sum_over_dp(total(sum_att))
    grad_mix = grad_att[:, :group].T
    grad_qkv = grad_att[:, group:].reshape(share, 3, group).transpose(1, 0, 2)
    grad_proj = sum_over_dp(proj_term).T
    return (
        layer_output,
        text_grad,
        feat_grad,
        grad_proj,
        grad_box,
        vectors[:2],
        grad_pos,
        vectors[2],
        vectors[3],
        grad_qkv,
        grad_mix,
        vectors[4],
        vectors[5],
        grad_up,
        grad_down,
        vectors[6],
        vectors[7],
    )


def solution(mesh):
    return jax.shard_map(
        local,
        mesh=mesh,
        in_specs=(
            P("dp", None, None),
            P("dp", "tensor"),
            P("dp", None),
            P("dp", None),
            P("dp"),
            P("dp", None, None),
            P("dp", None, None),
            P("tensor", None),
            P(),
            P(),
            P(),
            P(),
            P(),
            P(None, None, "tensor"),
            P("tensor", None),
            P(),
            P(),
            P(None, "tensor"),
            P("tensor", None),
            P(),
            P(),
            P("dp", None, None),
        ),
        out_specs=(
            P("dp", None, None),
            P("dp", None, None),
            P("dp", "tensor"),
            P("tensor", "dp"),
            P(None, "dp", None),
            P(None, "dp"),
            P("dp", None),
            P("dp"),
            P("dp"),
            P(None, "dp", "tensor"),
            P("tensor", "dp"),
            P("dp"),
            P("dp"),
            P("dp", "tensor"),
            P("tensor", "dp"),
            P("dp"),
            P("dp"),
        ),
        check_vma=False,
    )
```

```python
import jax
import jax.numpy as jnp
from jax import lax
from jax.experimental import pallas as pl
from jax.experimental.pallas import tpu as pltpu
from jax.sharding import PartitionSpec as P

HD = 64
LT = 384
EPSILON = 1e-06
NEGATIVE = -1000000000.0
BF = jnp.bfloat16
F32 = jnp.float32


def layer_norm(values, gain, bias):
    mean = jnp.mean(values, axis=-1, keepdims=True)
    centred = values - mean
    variance = jnp.mean(centred * centred, axis=-1, keepdims=True)
    inverse = lax.rsqrt(variance + EPSILON)
    normed = centred * inverse
    return (normed * gain + bias, normed, inverse)


def key_mask(seg_row, count):
    length = seg_row.shape[0]
    places = jnp.arange(length, dtype=jnp.int32)
    usable = places < LT + count
    same = seg_row[:, None] == seg_row[None, :]
    return same & (usable[None, :] | (places[:, None] == places[None, :]))


VMEM_BYTES = 52 << 20
ROOT_HALF = 0.7071067811865476
DENSITY = 0.3989422804014327


def dot(a, b):
    return jnp.dot(a, b, preferred_element_type=F32)


def dot_nt(a, b):
    return lax.dot_general(a, b, (((1,), (1,)), ((), ())), preferred_element_type=F32)


def dot_tn(a, b):
    return lax.dot_general(a, b, (((0,), (0,)), ((), ())), preferred_element_type=F32)


def any_specs(count):
    return [pl.BlockSpec(memory_space=pl.ANY)] * count


def smem_spec():
    return [pl.BlockSpec(memory_space=pltpu.SMEM)]


def vmem_specs(count):
    return [pl.BlockSpec(memory_space=pltpu.VMEM)] * count


def call(body, outs, in_specs, out_specs, scratch, flops):
    return pl.pallas_call(
        body,
        out_shape=[jax.ShapeDtypeStruct(shape, kind) for shape, kind in outs],
        in_specs=in_specs,
        out_specs=out_specs,
        scratch_shapes=scratch,
        compiler_params=pltpu.CompilerParams(vmem_limit_bytes=VMEM_BYTES),
        cost_estimate=pl.CostEstimate(flops=flops, bytes_accessed=16 << 20, transcendentals=0),
    )


def attend_kernel(heads, sizes, side_ref, x_ref, z_ref, allow_ref, *rest):
    count = len(sizes)
    shards, rest = regroup(rest, sizes)
    zout_ref, helds, lses = rest[0], rest[1 : 1 + count], rest[1 + count : 1 + 2 * count]
    weights, sems = rest[1 + 2 * count :]
    started, _ = fetch_shards(shards, weights, side_ref[0], sems)
    length, width = x_ref.shape
    group = heads * HD
    block = length
    lane = lax.broadcasted_iota(jnp.int32, (block, 128), 1)
    for i in range(count):
        for copy in started[i]:
            copy.wait()
        w_ref, held, lse_ref = weights.at[i], helds[i], lses[i]
        mixed = dot(x_ref[...], w_ref[...])
        held[:, group : 2 * group] = (mixed[:, group : 2 * group] * HD ** (-0.5)).astype(BF)
        held[:, 2 * group :] = mixed[:, 2 * group :].astype(BF)

        def rows(b, carry):
            at = pl.ds(pl.multiple_of(b * block, block), block)
            columns = jnp.zeros((block, 128), F32)
            allow = allow_ref[at, :] > 0.5
            for h in range(heads):
                q = held[at, group + h * HD : group + (h + 1) * HD]
                k = held[:, 2 * group + h * HD : 2 * group + (h + 1) * HD]
                v = held[:, 3 * group + h * HD : 3 * group + (h + 1) * HD]
                scores = jnp.where(allow, dot_nt(q, k), NEGATIVE)
                top = jnp.max(scores, axis=1, keepdims=True)
                raised = jnp.exp(scores - top)
                total = jnp.sum(raised, axis=1, keepdims=True)
                context = dot(raised.astype(BF), v) / total
                held[at, h * HD : (h + 1) * HD] = context.astype(BF)
                columns = jnp.where(lane == h, top + jnp.log(total), columns)
            lse_ref[:, at] = columns.T[:8, :]
            return carry

        for b in range(length // block):
            rows(b, 0)
        if i == 0:
            zout_ref[...] = z_ref[...] + dot_nt(held[:, :group], w_ref[:, :group])
        else:
            zout_ref[...] += dot_nt(held[:, :group], w_ref[:, :group])


def attend_call(heads, side, x, z, allow, shards):
    length, width = x.shape
    n = len(shards)
    sizes = [len(pieces) for pieces in shards]
    outs = [((length, width), F32)] + [((length, width), BF)] * n + [((8, length), F32)] * n
    got = call(
        lambda *refs: attend_kernel(heads, sizes, *refs),
        outs,
        smem_spec() + vmem_specs(3) + any_specs(sum(sizes)),
        vmem_specs(len(outs)),
        [pltpu.VMEM((n, width, width), BF), pltpu.SemaphoreType.DMA((sum(sizes),))],
        n * 2_000_000_000,
    )(side, x, z, allow, *sum(shards, []))
    return got[0], got[1 : 1 + n], got[1 + n :]


def attend_back_kernel(heads, sizes, side_ref, g_ref, gt_ref, xt_ref, acc_ref, allow_ref, *rest):
    count = len(sizes)
    shards, rest = regroup(rest, sizes)
    helds, lses = rest[:count], rest[count : 2 * count]
    accout_ref, terms = rest[2 * count], rest[2 * count + 1 : 3 * count + 1]
    gc_ref, grads, dq_ref, delta_ref, weights, full_ref, sems = rest[3 * count + 1 :]
    started, _ = fetch_shards(shards, weights, side_ref[0], sems)
    length, width = g_ref.shape
    group = heads * HD
    block = length
    lane = lax.broadcasted_iota(jnp.int32, (length, 128), 1)
    for i in range(count):
        for copy in started[i]:
            copy.wait()
        w_ref, held, lse_ref = weights.at[i], helds[i], lses[i]
        low = dot(g_ref[...], w_ref[:, :group]).astype(BF)
        gc_ref[...] = low
        product = low.astype(F32) * held[:, :group].astype(F32)
        columns = jnp.zeros((length, 128), F32)
        for h in range(heads):
            inner = jnp.sum(product[:, h * HD : (h + 1) * HD], axis=1, keepdims=True)
            columns = jnp.where(lane == h, inner, columns)
        delta_ref[...] = columns.T[:8, :]
        dq_ref[...] = jnp.zeros_like(dq_ref)
        grads[:, :group] = jnp.zeros((length, group), BF)

        def rows(b, carry):
            at = pl.ds(pl.multiple_of(b * block, block), block)
            allow = allow_ref[at, :] > 0.5
            for h in range(heads):
                q = held[:, group + h * HD : group + (h + 1) * HD]
                k = held[at, 2 * group + h * HD : 2 * group + (h + 1) * HD]
                v = held[at, 3 * group + h * HD : 3 * group + (h + 1) * HD]
                gc = gc_ref[:, h * HD : (h + 1) * HD]
                scores = jnp.where(allow, dot_nt(k, q), NEGATIVE)
                probs = jnp.exp(scores - lse_ref[h : h + 1, :])
                grad_probs = dot_nt(v, gc)
                grad_scores = (probs * (grad_probs - delta_ref[h : h + 1, :])).astype(BF)
                grads[at, 3 * group + h * HD : 3 * group + (h + 1) * HD] = dot(
                    probs.astype(BF), gc
                ).astype(BF)
                grads[at, 2 * group + h * HD : 2 * group + (h + 1) * HD] = dot(
                    grad_scores, q
                ).astype(BF)
                dq_ref[h * HD : (h + 1) * HD, :] += dot_tn(k, grad_scores)
            return carry

        for b in range(length // block):
            rows(b, 0)
        grads[:, group : 2 * group] = (dq_ref[...] * HD ** (-0.5)).T.astype(BF)
        if i == 0:
            accout_ref[...] = acc_ref[...] + dot_nt(grads[...], w_ref[...])
        else:
            accout_ref[...] += dot_nt(grads[...], w_ref[...])
        full_ref[...] = dot(xt_ref[...], grads[...]).astype(BF)
        full_ref[:, :group] = dot(gt_ref[...], held[:, :group]).astype(BF)
        store_blocks(terms[i], full_ref, side_ref[3])


def attend_back_call(heads, peers, side, g, gt, xt, acc, allow, shards, helds, lses):
    length, width = g.shape
    n = len(shards)
    sizes = [len(pieces) for pieces in shards]
    group = heads * HD
    outs = [((length, width), F32)] + [(blocks_shape(peers, width, width), BF)] * n
    got = call(
        lambda *refs: attend_back_kernel(heads, sizes, *refs),
        outs,
        smem_spec() + vmem_specs(5) + any_specs(sum(sizes)) + vmem_specs(2 * n),
        vmem_specs(len(outs)),
        [
            pltpu.VMEM((length, group), BF),
            pltpu.VMEM((length, width), BF),
            pltpu.VMEM((group, length), F32),
            pltpu.VMEM((8, length), F32),
            pltpu.VMEM((n, width, width), BF),
            pltpu.VMEM((width, width), BF),
            pltpu.SemaphoreType.DMA((sum(sizes),)),
        ],
        n * 4_000_000_000,
    )(side, g, gt, xt, acc, allow, *sum(shards, []), *helds, *lses)
    return got[0], got[1:]


def erf(x):
    x = jnp.clip(x, -4.0, 4.0)
    s = x * x
    top = jnp.full_like(x, -2.72614225801306e-10)
    for c in (
        2.77068142495902e-08,
        -2.10102402082508e-06,
        -5.69250639462346e-05,
        -7.34990630326855e-04,
        -2.95459980854025e-03,
        -1.60960333262415e-02,
    ):
        top = top * s + c
    base = jnp.full_like(x, -1.45660718464996e-05)
    for c in (
        -2.13374055278905e-04,
        -1.68282697438203e-03,
        -7.37332916720468e-03,
        -1.42647390514189e-02,
    ):
        base = base * s + c
    return x * top / base


def norm_back(grad, values, gain):
    _, normed, inverse = layer_norm(values, gain, 0.0)
    scaled = grad * gain
    mean_grad = jnp.mean(scaled, axis=-1, keepdims=True)
    mean_proj = jnp.mean(scaled * normed, axis=-1, keepdims=True)
    return (
        inverse * (scaled - mean_grad - normed * mean_proj),
        jnp.sum(grad * normed, axis=0, keepdims=True),
        jnp.sum(grad, axis=0, keepdims=True),
    )


def regroup(flat, sizes):
    flat = list(flat)
    return [[flat.pop(0) for _ in range(size)] for size in sizes], flat


def fetch_shards(shards, target, side, sems, base=0):
    started = []
    for i, pieces in enumerate(shards):
        copies = []
        for j, piece in enumerate(pieces):
            rows = piece.shape[0]
            at = pl.ds(pl.multiple_of((side if j == 0 else 1 - side) * rows, 16), rows)
            place = target.at[i] if len(pieces) == 1 else target.at[i, at]
            copies.append(pltpu.make_async_copy(piece, place, sems.at[base]))
            copies[-1].start()
            base += 1
        started.append(copies)
    return started, base


def forward_kernel(
    parts, sizes, side_ref, z_ref, cot_ref, gm_ref, bm_ref, gf_ref, bf_ref, *rest
):
    up_shards, rest = regroup(rest, sizes)
    down_shards, rest = regroup(rest, sizes)
    slope_any, terms = rest[0], rest[1 : parts + 1]
    out_ref, x1t_ref, gx2_ref, g_ref, vec_ref = rest[parts + 1 : parts + 6]
    ups, downs, actives, ffn_ref, x1_ref, gt_ref, slope_ref, held, sems = rest[parts + 6 :]
    up_started, down_started, base = [], [], 0
    for k in range(parts):
        copies, base = fetch_shards([up_shards[k]], ups.at[k : k + 1], side_ref[1], sems, base)
        up_started += copies
        copies, base = fetch_shards([down_shards[k]], downs.at[k : k + 1], side_ref[2], sems, base)
        down_started += copies
    leaving = []

    def leave(source, target):
        leaving.append(pltpu.make_async_copy(source, target, sems.at[base + len(leaving)]))
        leaving[-1].start()

    length, width = z_ref.shape
    block = 256
    vec_ref[...] = jnp.zeros_like(vec_ref)
    for b in range(length // block):
        at = slice(b * block, (b + 1) * block)
        hidden1, _, _ = layer_norm(z_ref[at, :], gm_ref[...], bm_ref[...])
        x1_ref[at, :] = hidden1.astype(BF)
        ffn_ref[at, :] = hidden1
        for k in range(parts):
            if b == 0:
                for copy in up_started[k]:
                    copy.wait()
            before = dot(x1_ref[at, :], ups[k])
            half = 0.5 + 0.5 * erf(before * ROOT_HALF)
            slope_ref[k, at, :] = (
                half + before * (DENSITY * jnp.exp(-0.5 * before * before))
            ).astype(BF)
            actives[k, at, :] = (before * half).astype(BF)
            if b == 0:
                for copy in down_started[k]:
                    copy.wait()
            ffn_ref[at, :] += dot(actives[k, at, :], downs[k])
            if at.stop == length:
                leave(slope_ref.at[k], slope_any.at[k])
        final, normed, inverse = layer_norm(ffn_ref[at, :], gf_ref[...], bf_ref[...])
        out_ref[at, :] = final.astype(BF)
        grad_in, gain_sum, bias_sum = norm_back(
            cot_ref[at, :].astype(F32), ffn_ref[at, :], gf_ref[...]
        )
        vec_ref[0:1, :] += gain_sum
        vec_ref[1:2, :] += bias_sum
        gx2_ref[at, :] = grad_in
        g_ref[at, :] = grad_in.astype(BF)
    gt_ref[...] = g_ref[...].T
    for k in sorted(range(parts), key=lambda k: (1 - k % 2, k)):
        store_blocks(held.at[k], dot(gt_ref[...], actives[k]).astype(BF), side_ref[3])
        leave(held.at[k], terms[k])
    x1t_ref[...] = x1_ref[...].T
    for copy in leaving:
        copy.wait()


def forward_call(peers, side, z, cot, gm, bm, gf, bf, up, down):
    length, width = z.shape
    n = len(up)
    sizes = [len(pieces) for pieces in up]
    inner = up[0][0].shape[1]
    shape = blocks_shape(peers, width, inner)
    outs = (
        [((n, length, inner), BF)]
        + [(shape, BF)] * n
        + [
            ((length, width), BF),
            ((width, length), BF),
            ((length, width), F32),
            ((length, width), BF),
            ((8, width), F32),
        ]
    )
    got = call(
        lambda *refs: forward_kernel(n, sizes, *refs),
        outs,
        smem_spec() + vmem_specs(6) + any_specs(2 * sum(sizes)),
        any_specs(n + 1) + vmem_specs(5),
        [
            pltpu.VMEM((n, width, inner), BF),
            pltpu.VMEM((n, inner, width), BF),
            pltpu.VMEM((n, length, inner), BF),
            pltpu.VMEM((length, width), F32),
            pltpu.VMEM((length, width), BF),
            pltpu.VMEM((width, length), BF),
            pltpu.VMEM((n, length, inner), BF),
            pltpu.VMEM((n, *shape), BF),
            pltpu.SemaphoreType.DMA((2 * sum(sizes) + 2 * n,)),
        ],
        8_000_000_000,
    )(side, z, cot, gm, bm, gf, bf, *sum(up, []), *sum(down, []))
    return got[0], got[1 : n + 1], got[n + 1 :]


def backward_kernel(
    parts, sizes, side_ref, z_ref, gx2_ref, g_ref, x1t_ref, gm_ref, *rest
):
    up_shards, rest = regroup(rest, sizes)
    down_shards, rest = regroup(rest, sizes)
    slope_any, *rest = rest
    terms = rest[:parts]
    gx1_ref, ga_ref, gat_ref, vec_ref, gb_ref, ups, downs, slopes, held, sems = rest[parts:]
    order = sorted(range(parts), key=lambda k: (1 - k % 2, k))
    started, base = {}, 0
    for k in order:
        first, base = fetch_shards([down_shards[k]], downs.at[k : k + 1], side_ref[2], sems, base)
        slope = pltpu.make_async_copy(slope_any.at[k], slopes.at[k], sems.at[base])
        slope.start()
        second, base = fetch_shards([up_shards[k]], ups.at[k : k + 1], side_ref[1], sems, base + 1)
        started[k] = first[0] + [slope], second[0]
    leaving = []
    gx1_ref[...] = gx2_ref[...]
    for k in order:
        for copy in started[k][0]:
            copy.wait()
        gb_ref[...] = (dot_nt(g_ref[...], downs[k]) * slopes[k].astype(F32)).astype(BF)
        store_blocks(held.at[k], dot(x1t_ref[...], gb_ref[...]).astype(BF), side_ref[3])
        leaving.append(pltpu.make_async_copy(held.at[k], terms[k], sems.at[base + len(leaving)]))
        leaving[-1].start()
        for copy in started[k][1]:
            copy.wait()
        gx1_ref[...] += dot_nt(gb_ref[...], ups[k])
    grad_in, gain_sum, bias_sum = norm_back(gx1_ref[...], z_ref[...], gm_ref[...])
    vec_ref[...] = jnp.zeros_like(vec_ref)
    vec_ref[0:1, :] = gain_sum
    vec_ref[1:2, :] = bias_sum
    gx1_ref[...] = grad_in
    ga_ref[...] = grad_in.astype(BF)
    gat_ref[...] = ga_ref[...].T
    for copy in leaving:
        copy.wait()


def backward_call(peers, side, z, gx2, g, x1t, gm, up, down, slope):
    length, width = z.shape
    n = len(up)
    sizes = [len(pieces) for pieces in up]
    inner = up[0][0].shape[1]
    shape = blocks_shape(peers, width, inner)
    outs = [(shape, BF)] * n + [
        ((length, width), F32),
        ((length, width), BF),
        ((width, length), BF),
        ((8, width), F32),
    ]
    got = call(
        lambda *refs: backward_kernel(n, sizes, *refs),
        outs,
        smem_spec() + vmem_specs(5) + any_specs(2 * sum(sizes) + 1),
        any_specs(n) + vmem_specs(4),
        [
            pltpu.VMEM((length, inner), BF),
            pltpu.VMEM((n, width, inner), BF),
            pltpu.VMEM((n, inner, width), BF),
            pltpu.VMEM((n, length, inner), BF),
            pltpu.VMEM((n, *shape), BF),
            pltpu.SemaphoreType.DMA((2 * sum(sizes) + 2 * n,)),
        ],
        8_000_000_000,
    )(side, z, gx2, g, x1t, gm, *sum(up, []), *sum(down, []), slope)
    return got[:n], got[n:]


def pack_kernel(mix_ref, qkv_ref, out_ref):
    group = mix_ref.shape[0]
    out_ref[:, :group] = mix_ref[...].T
    for c in range(qkv_ref.shape[0]):
        out_ref[:, (c + 1) * group : (c + 2) * group] = qkv_ref[c]


def store_blocks(ref, value, me):
    if len(ref.shape) == 2:
        ref[...] = value[...]
        return
    count, share, _ = ref.shape
    bits = count.bit_length() - 1
    for p in range(count):
        apart = p ^ me
        place = sum(((apart >> i) & 1) << (bits - 1 - i) for i in range(bits))
        ref[place] = value[p * share : (p + 1) * share, :]


def blocks_shape(peers, width, columns):
    share = width // peers
    return (peers, share, columns) if share % 16 == 0 else (width, columns)


def choose(index, count, step, source, store):
    for c in range(count):

        @pl.when(index == c)
        def _(c=c):
            store(source[:, c * step : (c + 1) * step])


def project_kernel(parts, mine_ref, feats_ref, w_ref, *rest):
    outs, full = rest[:parts], rest[parts]
    full[...] = dot(feats_ref[...], w_ref[...])
    step = outs[0].shape[1]
    for k, out in enumerate(outs):

        def store(value, out=out):
            out[...] = value.astype(out.dtype)

        choose(mine_ref[0] ^ k, parts, step, full, store)


def outgoing_kernel(parts, mine_ref, own_ref, near_ref, far_ref, box_ref, table_ref, pick_ref, out_ref, full, low):
    stored, chunk = own_ref.shape
    bins = table_ref.shape[1]
    places = lax.broadcasted_iota(jnp.int32, (stored, bins), 1)
    full[...] = jnp.zeros_like(full)
    spare = low.shape[1] - chunk
    lane = lax.broadcasted_iota(jnp.int32, (stored, spare), 1)
    codes = jnp.zeros((stored, spare), F32)
    for c in range(table_ref.shape[0]):
        corner = box_ref[:, c : c + 1]
        full[...] += dot((corner == places).astype(BF), table_ref[c])
        codes = jnp.where(lane == c, corner.astype(F32) + 1.0, codes)
    low[:, chunk:] = codes.astype(BF)

    def store(value):
        total = own_ref[...] + near_ref[...].astype(F32) + far_ref[...].astype(F32)
        low[:, :chunk] = (total + value).astype(BF)

    choose(mine_ref[0], parts, chunk, full, store)
    slots = out_ref.shape[0]
    regions = lax.broadcasted_iota(jnp.int32, (slots, stored), 1)
    out_ref[...] = dot((pick_ref[...] == regions).astype(BF), low[...]).astype(BF)


def place_kernel(pick_ref, rows_ref, out_ref):
    places = lax.broadcasted_iota(jnp.int32, (out_ref.shape[0], rows_ref.shape[0]), 0)
    chosen = (pick_ref[...] == places).astype(BF)
    out_ref[...] = dot(chosen, rows_ref[:, : out_ref.shape[1]]).astype(BF)


def place_feats_kernel(chunk, pick_ref, rows_ref, feats_ref, out_ref, codes_ref):
    places = lax.broadcasted_iota(jnp.int32, (out_ref.shape[0], feats_ref.shape[0]), 0)
    chosen = (pick_ref[...] == places).astype(BF)
    out_ref[...] = dot(chosen, feats_ref[...]).astype(BF)
    last = rows_ref.shape[1] - 128
    first = chunk - last
    codes_ref[...] = dot(chosen, rows_ref[:, last:]).T[first : first + 8, :]


def move_rows_kernel(pick_ref, rows_ref, out_ref):
    shape = (out_ref.shape[0], rows_ref.shape[0])
    places = lax.broadcasted_iota(jnp.int32, shape, 0)
    out_ref[...] = dot((pick_ref[...] == places).astype(BF), rows_ref[...])


def take_rows_kernel(pick_ref, rows_ref, out_ref):
    shape = (out_ref.shape[0], rows_ref.shape[0])
    places = lax.broadcasted_iota(jnp.int32, shape, 1)
    out_ref[...] = dot((pick_ref[...] == places).astype(BF), rows_ref[...]).astype(BF)


def embed_kernel(parts, text_ref, placed_ref, type_ref, pos_ref, gain_ref, bias_ref, emb_ref, hid_ref, x_ref, xt_ref):
    text_len = text_ref.shape[0]
    chunk = placed_ref.shape[2]
    types = type_ref[...].astype(F32)
    pos = pos_ref[...].astype(F32)
    emb_ref[:text_len, :] = text_ref[...].astype(F32) + types[0:1, :] + pos[:text_len, :]
    for c in range(parts):
        at = slice(c * chunk, (c + 1) * chunk)
        emb_ref[text_len:, at] = placed_ref[c].astype(F32)
    emb_ref[text_len:, :] += types[1:2, :] + pos[text_len:, :]
    hidden, _, _ = layer_norm(emb_ref[...], gain_ref[...], bias_ref[...])
    hid_ref[...] = hidden
    x_ref[...] = hidden.astype(BF)
    xt_ref[...] = x_ref[...].T


def embed_back_kernel(grad_ref, emb_ref, gain_ref, mid_ref, fin_ref, text_ref, reg_ref, vec):
    text_len = text_ref.shape[0]
    slots = emb_ref.shape[0] - text_len
    grad_in, gain_sum, bias_sum = norm_back(grad_ref[...], emb_ref[...], gain_ref[...])
    text_ref[...] = grad_in[:text_len, :].astype(BF)
    reg_ref[:slots, :] = grad_in[text_len:, :].astype(BF)
    vec[...] = jnp.zeros_like(vec)
    vec[0:1, :] = jnp.sum(grad_in[:text_len, :], axis=0, keepdims=True)
    vec[1:2, :] = jnp.sum(grad_in[text_len:, :], axis=0, keepdims=True)
    vec[2:3, :] = gain_sum
    vec[3:4, :] = bias_sum
    vec[4:6, :] = mid_ref[0:2, :]
    vec[6:8, :] = fin_ref[0:2, :]
    reg_ref[slots:, :] = vec[...].astype(BF)


def return_kernel(parts, mine_ref, pick_ref, feats_ref, codes_ref, w_ref, *rest):
    pieces = rest[:parts]
    wire_ref, proj_ref, box_ref, rest_ref, rows, columns, sums, full_ref = rest[parts:]
    slots = rows.shape[0] // parts
    chunk = columns.shape[1]
    for k in range(parts):
        rows[k * slots : (k + 1) * slots, :] = pieces[k][:slots, :]
    low = dot_nt(rows[...], w_ref[...]).astype(BF)
    places = lax.broadcasted_iota(jnp.int32, (wire_ref.shape[0], rows.shape[0]), 1)
    wire_ref[...] = dot((pick_ref[...] == places).astype(BF), low).astype(BF)
    full_ref[...] = dot(rows[...].T, feats_ref[...]).astype(BF)
    store_blocks(proj_ref, full_ref, mine_ref[1])
    sums[...] = pieces[0][...].astype(F32)
    for k in range(1, parts):
        sums[...] += pieces[k][...].astype(F32)

    def store_rows(value):
        columns[...] = value

    def store_rest(value):
        rest_ref[...] = value

    choose(mine_ref[0], parts, chunk, rows, store_rows)
    choose(mine_ref[0], parts, chunk, sums, store_rest)
    bins = box_ref.shape[1]
    codes = lax.broadcasted_iota(jnp.int32, (bins, rows.shape[0]), 0).astype(F32) + 1.0
    for c in range(box_ref.shape[0]):
        box_ref[c] = dot((codes_ref[c : c + 1, :] == codes).astype(BF), columns[...])


def text_kernel(parts, mine_ref, *rest):
    pieces, (out_ref, pos_ref, sums) = rest[:parts], rest[parts:]
    sums[...] = pieces[0][...].astype(F32)
    out_ref[mine_ref[0]] = sums[...]
    for k in range(1, parts):
        value = pieces[k][...].astype(F32)
        out_ref[mine_ref[0] ^ k] = value
        sums[...] += value

    def store(value):
        pos_ref[...] = value

    choose(mine_ref[0], parts, pos_ref.shape[1], sums, store)


def line_up_kernel(parts, mine_ref, *rest):
    pieces, out_ref = rest[:parts], rest[parts]
    for k in range(parts):
        out_ref[mine_ref[0] ^ k] = pieces[k][...]


def spread_kernel(parts, chunks_ref, out_ref):
    chunk = chunks_ref.shape[2]
    for c in range(parts):
        out_ref[:, c * chunk : (c + 1) * chunk] = chunks_ref[c]


def small_call(body, args, outs, scratch=(), scalar=False, flops=500_000_000):
    specs = vmem_specs(len(args))
    if scalar:
        specs[0] = pl.BlockSpec(memory_space=pltpu.SMEM)
    got = call(body, outs, specs, vmem_specs(len(outs)), list(scratch), flops)(*args)
    return got[0] if len(outs) == 1 else got


def swap(value, axis, bit):
    count = lax.axis_size(axis)
    return lax.ppermute(value, axis, [(i, i ^ bit) for i in range(count)])


def bits_of(axis):
    count = lax.axis_size(axis)
    return [1 << i for i in range(count.bit_length() - 1)]


def tie(first, second):
    return lax.optimization_barrier((first, second))


def far_half(shard, bit):
    rows = shard.shape[0] // 2
    side = (lax.axis_index("dp") // bit) % 2
    return swap(lax.dynamic_slice_in_dim(shard, side * rows, rows, 0), "tensor", 2)


def gather_shards(shard, half, other):
    return [
        [shard],
        [swap(shard, "tensor", 1)],
        [half, other],
        [swap(half, "tensor", 1), swap(other, "tensor", 1)],
    ]


def pair_sum(terms):
    here = [terms[0], swap(terms[1], "tensor", 1)]
    return here, total([terms[2], swap(terms[3], "tensor", 1)]).astype(BF)


def total(summands):
    return sum(value.astype(F32) for value in summands)


def sum_over_dp(values):
    bits = bits_of("dp")
    if values[0].ndim == 2:
        term = total(values).astype(BF)
        term = term.reshape(1 << len(bits), -1, term.shape[1])
        return jnp.sum(lax.all_to_all(term, "dp", 0, 0, tiled=True).astype(F32), axis=0)
    for bit in bits:
        half = values[0].shape[0] // 2
        sent = total([v[half:] for v in values]).astype(BF)
        values = [v[:half] for v in values] + [swap(sent, "dp", bit)]
    return total(values)[0]


def local(
    text_embed,
    region_feats,
    box_coords,
    seg_ids,
    region_counts,
    send_index,
    recv_pos,
    w_proj,
    box_table,
    type_embed,
    pos_embed,
    gain_embed,
    bias_embed,
    w_qkv,
    w_mix,
    gain_mid,
    bias_mid,
    w_up,
    w_down,
    gain_final,
    bias_final,
    cotangent,
):
    parts = lax.axis_size("tensor")
    peers = lax.axis_size("dp")
    mine = lax.axis_index("tensor")
    dp_now = lax.axis_index("dp")
    mine_now = jnp.stack([mine, dp_now]).astype(jnp.int32)
    sides = jnp.stack([dp_now % 2, dp_now % 2, (dp_now // 2) % 2, dp_now]).astype(jnp.int32)
    row_count, text_len, width = text_embed.shape
    assert row_count == parts == 4
    length = seg_ids.shape[1]
    slots = length - text_len
    stored, depth = region_feats.shape
    capacity = send_index.shape[2]
    bins = box_table.shape[1]
    group = w_qkv.shape[2]
    heads = group // HD
    chunk = width // parts
    share = width // peers
    broad = -(-(chunk + 8) // 128) * 128
    wire = peers * capacity

    def own(array):
        return lax.dynamic_index_in_dim(array, mine, 0, keepdims=False)

    def line(vector):
        return vector.reshape(1, width)

    held = small_call(
        lambda *refs: project_kernel(parts, *refs),
        [mine_now, region_feats, w_proj],
        [((stored, chunk), F32 if k == 0 else BF) for k in range(parts)],
        [pltpu.VMEM((stored, width), F32)],
        scalar=True,
    )
    near = swap(held[1], "tensor", 1)
    across = (held[2].astype(F32) + swap(held[3], "tensor", 1).astype(F32)).astype(BF)

    across, (w_mix, w_qkv) = tie(across, (w_mix, w_qkv))
    far = swap(across, "tensor", 2)
    packed = small_call(pack_kernel, [w_mix, w_qkv], [((width, width), BF)])
    far, packed = tie(far, packed)
    att_half = far_half(packed, 1)

    send_flat = send_index.reshape(-1)
    recv_flat = recv_pos.reshape(-1)
    recv_slot = jnp.where(
        recv_flat >= 0,
        (recv_flat // length) * slots + recv_flat % length - text_len,
        -1,
    )
    recv_near = jnp.where(recv_flat >= 0, (recv_slot // slots ^ mine) * slots + recv_slot % slots, -1)
    near_line, near_column = recv_near.reshape(1, wire), recv_near.reshape(wire, 1)
    send_line, send_column = send_flat.reshape(1, wire), send_flat.reshape(wire, 1)
    recv_line = recv_slot.reshape(1, wire)
    outgoing = small_call(
        lambda *refs: outgoing_kernel(parts, *refs),
        [mine_now, held[0], near, far, box_coords, box_table, send_column],
        [((wire, broad), BF)],
        [pltpu.VMEM((stored, width), F32), pltpu.VMEM((stored, broad), BF)],
        scalar=True,
    )
    outgoing, w_up = tie(outgoing, w_up)
    up_half = far_half(w_up, 1)
    incoming = lax.all_to_all(
        outgoing.reshape(peers, capacity, broad), "dp", 0, 0, tiled=True
    ).reshape(wire, broad)
    incoming, att_half = tie(incoming, att_half)
    att_other = swap(att_half, "dp", 1)
    placed = small_call(
        place_kernel, [recv_line, incoming], [((row_count * slots, chunk), BF)]
    )
    placed = lax.all_to_all(placed.reshape(parts, slots, chunk), "tensor", 0, 0, tiled=True)
    placed, w_down = tie(placed, w_down)
    down_half = far_half(w_down, 2)

    embedded, hidden0, inputs0, inputs0_turned = small_call(
        lambda *refs: embed_kernel(parts, *refs),
        [own(text_embed), placed, type_embed, pos_embed, line(gain_embed), line(bias_embed)],
        [
            ((length, width), F32),
            ((length, width), F32),
            ((length, width), BF),
            ((width, length), BF),
        ],
    )
    (hidden0, inputs0), feats = tie((hidden0, inputs0), region_feats)
    feats_wire = small_call(take_rows_kernel, [send_column, feats], [((wire, depth), BF)])
    feats_wire = lax.all_to_all(
        feats_wire.reshape(peers, capacity, depth), "dp", 0, 0, tiled=True
    ).reshape(wire, depth)
    allowed = key_mask(own(seg_ids), own(region_counts))
    allow = allowed.astype(F32)
    allow_turned = allowed.T.astype(F32)

    (hidden0, inputs0), (up_half, att_other) = tie((hidden0, inputs0), (up_half, att_other))
    up_other = swap(up_half, "dp", 1)
    att_shards = gather_shards(packed, att_half, att_other)
    z, near_helds, near_lses = attend_call(heads, sides, inputs0, hidden0, allow, att_shards[:2])
    z, (up_other, down_half) = tie(z, (up_other, down_half))
    down_other = swap(down_half, "dp", 2)
    up = gather_shards(w_up, up_half, up_other)
    z, far_helds, far_lses = attend_call(heads, sides, inputs0, z, allow, att_shards[2:])
    helds, lses = near_helds + far_helds, near_lses + far_lses
    z, down_other = tie(z, down_other)
    down = gather_shards(w_down, down_half, down_other)
    slopes, down_terms, (final, x1t, grad_x2, grad_ffn, final_vectors) = forward_call(
        peers,
        sides,
        z,
        own(cotangent),
        line(gain_mid),
        line(bias_mid),
        line(gain_final),
        line(bias_final),
        up,
        down,
    )
    down_here, down_across = pair_sum(down_terms)
    final_far = swap(final, "tensor", 2)

    up_terms, (grad_x1, grad_attn, grad_attn_turned, mid_vectors) = backward_call(
        peers, sides, z, grad_x2, grad_ffn, x1t, line(gain_mid), up, down, slopes
    )
    (grad_attn, grad_x1), (down_across, final_far, feats_wire) = tie(
        (grad_attn, grad_x1), (down_across, final_far, feats_wire)
    )
    down_far = swap(down_across, "tensor", 2)
    up_here, up_across = pair_sum(up_terms)
    slot_feats, slot_codes = small_call(
        lambda *refs: place_feats_kernel(chunk, *refs),
        [near_line, incoming, feats_wire],
        [((row_count * slots, depth), BF), ((8, row_count * slots), F32)],
    )
    total0 = grad_x1
    att_terms = [None] * parts
    for at in (1, 0):
        picked = range(at, parts, 2)
        total0, terms = attend_back_call(
            heads,
            peers,
            sides,
            grad_attn,
            grad_attn_turned,
            inputs0_turned,
            total0,
            allow_turned,
            [att_shards[k] for k in picked],
            [helds[k] for k in picked],
            [lses[k] for k in picked],
        )
        for k, term in zip(picked, terms, strict=True):
            att_terms[k] = term
        if at:
            total0, (up_across, slot_feats) = tie(total0, (up_across, slot_feats))
            up_far = swap(up_across, "tensor", 2)
    total0, down_far = tie(total0, down_far)
    att_here, att_across = pair_sum(att_terms)

    def neighbours(piece, far):
        return [piece, swap(piece, "tensor", 1), far, swap(far, "tensor", 1)]

    text_own, regions_own = small_call(
        embed_back_kernel,
        [total0, embedded, line(gain_embed), mid_vectors, final_vectors],
        [((text_len, width), BF), ((slots + 16, width), BF)],
        [pltpu.VMEM((16, width), F32)],
    )
    regions_far = swap(regions_own, "tensor", 2)
    regions_far, (text_own, att_across) = tie(regions_far, (text_own, att_across))
    att_far = swap(att_across, "tensor", 2)
    text_far = swap(text_own, "tensor", 2)
    feats_back, proj_term, box_term, rest_sum = small_call(
        lambda *refs: return_kernel(parts, *refs),
        [mine_now, near_column, slot_feats, slot_codes, w_proj]
        + neighbours(regions_own, regions_far),
        [
            ((wire, depth), BF),
            (blocks_shape(peers, width, depth), BF),
            ((box_table.shape[0], bins, chunk), F32),
            ((slots + 16, chunk), F32),
        ],
        [
            pltpu.VMEM((row_count * slots, width), BF),
            pltpu.VMEM((row_count * slots, chunk), BF),
            pltpu.VMEM((slots + 16, width), F32),
            pltpu.VMEM((width, depth), BF),
        ],
        scalar=True,
    )
    feats_back = lax.all_to_all(
        feats_back.reshape(peers, capacity, depth), "dp", 0, 0, tiled=True
    ).reshape(wire, depth)
    feat_grad = small_call(move_rows_kernel, [send_line, feats_back], [((stored, depth), F32)])
    text_grad, text_sum = small_call(
        lambda *refs: text_kernel(parts, *refs),
        [mine_now] + neighbours(text_own, text_far),
        [((parts, text_len, width), F32), ((text_len, chunk), F32)],
        [pltpu.VMEM((text_len, width), F32)],
        scalar=True,
    )
    layer_output = small_call(
        lambda *refs: line_up_kernel(parts, *refs),
        [mine_now] + neighbours(final, final_far),
        [((parts, length, width), BF)],
        scalar=True,
    )
    pos_term = jnp.concatenate([text_sum, rest_sum[:slots]], axis=0)
    bin_share = bins // peers
    pos_share = length // peers
    bundle = jnp.concatenate(
        [
            pos_term.reshape(peers, pos_share, chunk),
            box_term.reshape(-1, peers, bin_share, chunk)
            .transpose(1, 0, 2, 3)
            .reshape(peers, -1, chunk),
            jnp.broadcast_to(rest_sum[slots:], (peers, 16, chunk)),
        ],
        axis=1,
    ).astype(BF)
    bundle = jnp.sum(
        lax.all_to_all(bundle, "dp", 0, 0, tiled=True).astype(F32), axis=0
    )
    bundle = lax.all_gather(bundle, "tensor", axis=0, tiled=False)
    bundle = small_call(
        lambda *refs: spread_kernel(parts, *refs), [bundle], [((bundle.shape[1], width), F32)]
    )
    grad_pos = bundle[:pos_share]
    grad_box = bundle[pos_share:-16].reshape(-1, bin_share, width)
    vectors = lax.dynamic_slice_in_dim(bundle[-16:], lax.axis_index("dp") * share, share, 1)

    grad_down = sum_over_dp(down_here + [down_far]).T
    grad_up = sum_over_dp(up_here + [up_far])
    grad_att = sum_over_dp(att_here + [att_far])
    grad_mix = grad_att[:, :group].T
    grad_qkv = grad_att[:, group:].reshape(share, 3, group).transpose(1, 0, 2)
    grad_proj = sum_over_dp([proj_term]).T
    return (
        layer_output,
        text_grad,
        feat_grad,
        grad_proj,
        grad_box,
        vectors[:2],
        grad_pos,
        vectors[2],
        vectors[3],
        grad_qkv,
        grad_mix,
        vectors[4],
        vectors[5],
        grad_up,
        grad_down,
        vectors[6],
        vectors[7],
    )


def solution(mesh):
    return jax.shard_map(
        local,
        mesh=mesh,
        in_specs=(
            P("dp", None, None),
            P("dp", "tensor"),
            P("dp", None),
            P("dp", None),
            P("dp"),
            P("dp", None, None),
            P("dp", None, None),
            P("tensor", None),
            P(),
            P(),
            P(),
            P(),
            P(),
            P(None, None, "tensor"),
            P("tensor", None),
            P(),
            P(),
            P(None, "tensor"),
            P("tensor", None),
            P(),
            P(),
            P("dp", None, None),
        ),
        out_specs=(
            P("dp", None, None),
            P("dp", None, None),
            P("dp", "tensor"),
            P("tensor", "dp"),
            P(None, "dp", None),
            P(None, "dp"),
            P("dp", None),
            P("dp"),
            P("dp"),
            P(None, "dp", "tensor"),
            P("tensor", "dp"),
            P("dp"),
            P("dp"),
            P("dp", "tensor"),
            P("tensor", "dp"),
            P("dp"),
            P("dp"),
        ),
        check_vma=False,
    )
```

```python
import jax
import jax.numpy as jnp
from jax import lax
from jax.experimental import pallas as pl
from jax.experimental.pallas import tpu as pltpu
from jax.sharding import PartitionSpec as P

HD = 64
LT = 384
EPSILON = 1e-06
NEGATIVE = -1000000000.0
BF = jnp.bfloat16
F32 = jnp.float32


def layer_norm(values, gain, bias):
    mean = jnp.mean(values, axis=-1, keepdims=True)
    centred = values - mean
    variance = jnp.mean(centred * centred, axis=-1, keepdims=True)
    inverse = lax.rsqrt(variance + EPSILON)
    normed = centred * inverse
    return (normed * gain + bias, normed, inverse)


def key_mask(seg_row, count):
    length = seg_row.shape[0]
    places = jnp.arange(length, dtype=jnp.int32)
    usable = places < LT + count
    same = seg_row[:, None] == seg_row[None, :]
    return same & (usable[None, :] | (places[:, None] == places[None, :]))


VMEM_BYTES = 52 << 20
ROOT_HALF = 0.7071067811865476
DENSITY = 0.3989422804014327


def dot(a, b):
    return jnp.dot(a, b, preferred_element_type=F32)


def dot_nt(a, b):
    return lax.dot_general(a, b, (((1,), (1,)), ((), ())), preferred_element_type=F32)


def dot_tn(a, b):
    return lax.dot_general(a, b, (((0,), (0,)), ((), ())), preferred_element_type=F32)


def any_specs(count):
    return [pl.BlockSpec(memory_space=pl.ANY)] * count


def smem_spec():
    return [pl.BlockSpec(memory_space=pltpu.SMEM)]


def vmem_specs(count):
    return [pl.BlockSpec(memory_space=pltpu.VMEM)] * count


def call(body, outs, in_specs, out_specs, scratch, flops, moved=16 << 20):
    return pl.pallas_call(
        body,
        out_shape=[jax.ShapeDtypeStruct(shape, kind) for shape, kind in outs],
        in_specs=in_specs,
        out_specs=out_specs,
        scratch_shapes=scratch,
        compiler_params=pltpu.CompilerParams(vmem_limit_bytes=VMEM_BYTES),
        cost_estimate=pl.CostEstimate(flops=flops, bytes_accessed=moved, transcendentals=0),
    )


def attend_kernel(heads, sizes, side_ref, x_ref, z_ref, allow_ref, *rest):
    count = len(sizes)
    shards, rest = regroup(rest, sizes)
    zout_ref, helds, lses = rest[0], rest[1 : 1 + count], rest[1 + count : 1 + 2 * count]
    weights, sems = rest[1 + 2 * count :]
    started, _ = fetch_shards(shards, weights, side_ref[0], sems)
    length, width = x_ref.shape
    group = heads * HD
    block = length
    lane = lax.broadcasted_iota(jnp.int32, (block, 128), 1)
    for i in range(count):
        for copy in started[i]:
            copy.wait()
        w_ref, held, lse_ref = weights.at[i], helds[i], lses[i]
        mixed = dot(x_ref[...], w_ref[...])
        held[:, group : 2 * group] = (mixed[:, group : 2 * group] * HD ** (-0.5)).astype(BF)
        held[:, 2 * group :] = mixed[:, 2 * group :].astype(BF)

        def rows(b, carry):
            at = pl.ds(pl.multiple_of(b * block, block), block)
            columns = jnp.zeros((block, 128), F32)
            allow = allow_ref[at, :] > 0.5
            for h in range(heads):
                q = held[at, group + h * HD : group + (h + 1) * HD]
                k = held[:, 2 * group + h * HD : 2 * group + (h + 1) * HD]
                v = held[:, 3 * group + h * HD : 3 * group + (h + 1) * HD]
                scores = jnp.where(allow, dot_nt(q, k), NEGATIVE)
                top = jnp.max(scores, axis=1, keepdims=True)
                raised = jnp.exp(scores - top)
                total = jnp.sum(raised, axis=1, keepdims=True)
                context = dot(raised.astype(BF), v) / total
                held[at, h * HD : (h + 1) * HD] = context.astype(BF)
                columns = jnp.where(lane == h, top + jnp.log(total), columns)
            lse_ref[:, at] = columns.T[:8, :]
            return carry

        for b in range(length // block):
            rows(b, 0)
        if i == 0:
            zout_ref[...] = z_ref[...] + dot_nt(held[:, :group], w_ref[:, :group])
        else:
            zout_ref[...] += dot_nt(held[:, :group], w_ref[:, :group])


def attend_call(heads, side, x, z, allow, shards):
    length, width = x.shape
    n = len(shards)
    sizes = [len(pieces) for pieces in shards]
    outs = [((length, width), F32)] + [((length, width), BF)] * n + [((8, length), F32)] * n
    got = call(
        lambda *refs: attend_kernel(heads, sizes, *refs),
        outs,
        smem_spec() + vmem_specs(3) + any_specs(sum(sizes)),
        vmem_specs(len(outs)),
        [pltpu.VMEM((n, width, width), BF), pltpu.SemaphoreType.DMA((sum(sizes),))],
        n * 2_000_000_000,
    )(side, x, z, allow, *sum(shards, []))
    return got[0], got[1 : 1 + n], got[1 + n :]


def attend_back_kernel(heads, sizes, side_ref, g_ref, gt_ref, xt_ref, acc_ref, allow_ref, *rest):
    count = len(sizes)
    shards, rest = regroup(rest, sizes)
    helds, lses = rest[:count], rest[count : 2 * count]
    accout_ref, terms = rest[2 * count], rest[2 * count + 1 : 3 * count + 1]
    gc_ref, grads, dq_ref, delta_ref, weights, full_ref, sems = rest[3 * count + 1 :]
    started, _ = fetch_shards(shards, weights, side_ref[0], sems)
    length, width = g_ref.shape
    group = heads * HD
    block = length
    lane = lax.broadcasted_iota(jnp.int32, (length, 128), 1)
    for i in range(count):
        for copy in started[i]:
            copy.wait()
        w_ref, held, lse_ref = weights.at[i], helds[i], lses[i]
        low = dot(g_ref[...], w_ref[:, :group]).astype(BF)
        gc_ref[...] = low
        product = low.astype(F32) * held[:, :group].astype(F32)
        columns = jnp.zeros((length, 128), F32)
        for h in range(heads):
            inner = jnp.sum(product[:, h * HD : (h + 1) * HD], axis=1, keepdims=True)
            columns = jnp.where(lane == h, inner, columns)
        delta_ref[...] = columns.T[:8, :]
        dq_ref[...] = jnp.zeros_like(dq_ref)
        grads[:, :group] = jnp.zeros((length, group), BF)

        def rows(b, carry):
            at = pl.ds(pl.multiple_of(b * block, block), block)
            allow = allow_ref[at, :] > 0.5
            for h in range(heads):
                q = held[:, group + h * HD : group + (h + 1) * HD]
                k = held[at, 2 * group + h * HD : 2 * group + (h + 1) * HD]
                v = held[at, 3 * group + h * HD : 3 * group + (h + 1) * HD]
                gc = gc_ref[:, h * HD : (h + 1) * HD]
                scores = jnp.where(allow, dot_nt(k, q), NEGATIVE)
                probs = jnp.exp(scores - lse_ref[h : h + 1, :])
                grad_probs = dot_nt(v, gc)
                grad_scores = (probs * (grad_probs - delta_ref[h : h + 1, :])).astype(BF)
                grads[at, 3 * group + h * HD : 3 * group + (h + 1) * HD] = dot(
                    probs.astype(BF), gc
                ).astype(BF)
                grads[at, 2 * group + h * HD : 2 * group + (h + 1) * HD] = dot(
                    grad_scores, q
                ).astype(BF)
                dq_ref[h * HD : (h + 1) * HD, :] += dot_tn(k, grad_scores)
            return carry

        for b in range(length // block):
            rows(b, 0)
        grads[:, group : 2 * group] = (dq_ref[...] * HD ** (-0.5)).T.astype(BF)
        if i == 0:
            accout_ref[...] = acc_ref[...] + dot_nt(grads[...], w_ref[...])
        else:
            accout_ref[...] += dot_nt(grads[...], w_ref[...])
        full_ref[...] = dot(xt_ref[...], grads[...]).astype(BF)
        full_ref[:, :group] = dot(gt_ref[...], held[:, :group]).astype(BF)
        store_blocks(terms[i], full_ref, side_ref[3])


def attend_back_call(heads, peers, side, g, gt, xt, acc, allow, shards, helds, lses):
    length, width = g.shape
    n = len(shards)
    sizes = [len(pieces) for pieces in shards]
    group = heads * HD
    outs = [((length, width), F32)] + [(blocks_shape(peers, width, width), BF)] * n
    got = call(
        lambda *refs: attend_back_kernel(heads, sizes, *refs),
        outs,
        smem_spec() + vmem_specs(5) + any_specs(sum(sizes)) + vmem_specs(2 * n),
        vmem_specs(len(outs)),
        [
            pltpu.VMEM((length, group), BF),
            pltpu.VMEM((length, width), BF),
            pltpu.VMEM((group, length), F32),
            pltpu.VMEM((8, length), F32),
            pltpu.VMEM((n, width, width), BF),
            pltpu.VMEM((width, width), BF),
            pltpu.SemaphoreType.DMA((sum(sizes),)),
        ],
        n * 4_000_000_000,
    )(side, g, gt, xt, acc, allow, *sum(shards, []), *helds, *lses)
    return got[0], got[1:]


def erf(x):
    x = jnp.clip(x, -4.0, 4.0)
    s = x * x
    top = jnp.full_like(x, -2.72614225801306e-10)
    for c in (
        2.77068142495902e-08,
        -2.10102402082508e-06,
        -5.69250639462346e-05,
        -7.34990630326855e-04,
        -2.95459980854025e-03,
        -1.60960333262415e-02,
    ):
        top = top * s + c
    base = jnp.full_like(x, -1.45660718464996e-05)
    for c in (
        -2.13374055278905e-04,
        -1.68282697438203e-03,
        -7.37332916720468e-03,
        -1.42647390514189e-02,
    ):
        base = base * s + c
    return x * top / base


def norm_back(grad, values, gain):
    _, normed, inverse = layer_norm(values, gain, 0.0)
    scaled = grad * gain
    mean_grad = jnp.mean(scaled, axis=-1, keepdims=True)
    mean_proj = jnp.mean(scaled * normed, axis=-1, keepdims=True)
    return (
        inverse * (scaled - mean_grad - normed * mean_proj),
        jnp.sum(grad * normed, axis=0, keepdims=True),
        jnp.sum(grad, axis=0, keepdims=True),
    )


def regroup(flat, sizes):
    flat = list(flat)
    return [[flat.pop(0) for _ in range(size)] for size in sizes], flat


def fetch_shards(shards, target, side, sems, base=0):
    started = []
    for i, pieces in enumerate(shards):
        copies = []
        for j, piece in enumerate(pieces):
            rows = piece.shape[0]
            at = pl.ds(pl.multiple_of((side if j == 0 else 1 - side) * rows, 16), rows)
            place = target.at[i] if len(pieces) == 1 else target.at[i, at]
            copies.append(pltpu.make_async_copy(piece, place, sems.at[base]))
            copies[-1].start()
            base += 1
        started.append(copies)
    return started, base


def forward_kernel(
    parts, sizes, side_ref, z_ref, cot_ref, gm_ref, bm_ref, gf_ref, bf_ref, *rest
):
    up_shards, rest = regroup(rest, sizes)
    down_shards, rest = regroup(rest, sizes)
    slope_any, terms = rest[0], rest[1 : parts + 1]
    out_ref, x1t_ref, gx2_ref, g_ref, vec_ref = rest[parts + 1 : parts + 6]
    ups, downs, actives, ffn_ref, x1_ref, gt_ref, slope_ref, held, sems = rest[parts + 6 :]
    up_started, down_started, base = [], [], 0
    for k in range(parts):
        copies, base = fetch_shards([up_shards[k]], ups.at[k : k + 1], side_ref[1], sems, base)
        up_started += copies
        copies, base = fetch_shards([down_shards[k]], downs.at[k : k + 1], side_ref[2], sems, base)
        down_started += copies
    leaving = []

    def leave(source, target):
        leaving.append(pltpu.make_async_copy(source, target, sems.at[base + len(leaving)]))
        leaving[-1].start()

    length, width = z_ref.shape
    block = 256
    vec_ref[...] = jnp.zeros_like(vec_ref)
    for b in range(length // block):
        at = slice(b * block, (b + 1) * block)
        hidden1, _, _ = layer_norm(z_ref[at, :], gm_ref[...], bm_ref[...])
        x1_ref[at, :] = hidden1.astype(BF)
        ffn_ref[at, :] = hidden1
        for k in range(parts):
            if b == 0:
                for copy in up_started[k]:
                    copy.wait()
            before = dot(x1_ref[at, :], ups[k])
            half = 0.5 + 0.5 * erf(before * ROOT_HALF)
            slope_ref[k, at, :] = (
                half + before * (DENSITY * jnp.exp(-0.5 * before * before))
            ).astype(BF)
            actives[k, at, :] = (before * half).astype(BF)
            if b == 0:
                for copy in down_started[k]:
                    copy.wait()
            ffn_ref[at, :] += dot(actives[k, at, :], downs[k])
            if at.stop == length:
                leave(slope_ref.at[k], slope_any.at[k])
        final, normed, inverse = layer_norm(ffn_ref[at, :], gf_ref[...], bf_ref[...])
        out_ref[at, :] = final.astype(BF)
        grad_in, gain_sum, bias_sum = norm_back(
            cot_ref[at, :].astype(F32), ffn_ref[at, :], gf_ref[...]
        )
        vec_ref[0:1, :] += gain_sum
        vec_ref[1:2, :] += bias_sum
        gx2_ref[at, :] = grad_in
        g_ref[at, :] = grad_in.astype(BF)
    gt_ref[...] = g_ref[...].T
    for k in sorted(range(parts), key=lambda k: (1 - k % 2, k)):
        store_blocks(held.at[k], dot(gt_ref[...], actives[k]).astype(BF), side_ref[3])
        leave(held.at[k], terms[k])
    x1t_ref[...] = x1_ref[...].T
    for copy in leaving:
        copy.wait()


def forward_call(peers, side, z, cot, gm, bm, gf, bf, up, down):
    length, width = z.shape
    n = len(up)
    sizes = [len(pieces) for pieces in up]
    inner = up[0][0].shape[1]
    shape = blocks_shape(peers, width, inner)
    outs = (
        [((n, length, inner), BF)]
        + [(shape, BF)] * n
        + [
            ((length, width), BF),
            ((width, length), BF),
            ((length, width), F32),
            ((length, width), BF),
            ((8, width), F32),
        ]
    )
    got = call(
        lambda *refs: forward_kernel(n, sizes, *refs),
        outs,
        smem_spec() + vmem_specs(6) + any_specs(2 * sum(sizes)),
        any_specs(n + 1) + vmem_specs(5),
        [
            pltpu.VMEM((n, width, inner), BF),
            pltpu.VMEM((n, inner, width), BF),
            pltpu.VMEM((n, length, inner), BF),
            pltpu.VMEM((length, width), F32),
            pltpu.VMEM((length, width), BF),
            pltpu.VMEM((width, length), BF),
            pltpu.VMEM((n, length, inner), BF),
            pltpu.VMEM((n, *shape), BF),
            pltpu.SemaphoreType.DMA((2 * sum(sizes) + 2 * n,)),
        ],
        8_000_000_000,
    )(side, z, cot, gm, bm, gf, bf, *sum(up, []), *sum(down, []))
    return got[0], got[1 : n + 1], got[n + 1 :]


def backward_kernel(
    parts, sizes, side_ref, z_ref, gx2_ref, g_ref, x1t_ref, gm_ref, *rest
):
    up_shards, rest = regroup(rest, sizes)
    down_shards, rest = regroup(rest, sizes)
    slope_any, *rest = rest
    terms = rest[:parts]
    gx1_ref, ga_ref, gat_ref, vec_ref, gb_ref, ups, downs, slopes, held, sems = rest[parts:]
    order = sorted(range(parts), key=lambda k: (1 - k % 2, k))
    started, base = {}, 0
    for k in order:
        first, base = fetch_shards([down_shards[k]], downs.at[k : k + 1], side_ref[2], sems, base)
        slope = pltpu.make_async_copy(slope_any.at[k], slopes.at[k], sems.at[base])
        slope.start()
        second, base = fetch_shards([up_shards[k]], ups.at[k : k + 1], side_ref[1], sems, base + 1)
        started[k] = first[0] + [slope], second[0]
    leaving = []
    gx1_ref[...] = gx2_ref[...]
    for k in order:
        for copy in started[k][0]:
            copy.wait()
        gb_ref[...] = (dot_nt(g_ref[...], downs[k]) * slopes[k].astype(F32)).astype(BF)
        store_blocks(held.at[k], dot(x1t_ref[...], gb_ref[...]).astype(BF), side_ref[3])
        leaving.append(pltpu.make_async_copy(held.at[k], terms[k], sems.at[base + len(leaving)]))
        leaving[-1].start()
        for copy in started[k][1]:
            copy.wait()
        gx1_ref[...] += dot_nt(gb_ref[...], ups[k])
    grad_in, gain_sum, bias_sum = norm_back(gx1_ref[...], z_ref[...], gm_ref[...])
    vec_ref[...] = jnp.zeros_like(vec_ref)
    vec_ref[0:1, :] = gain_sum
    vec_ref[1:2, :] = bias_sum
    gx1_ref[...] = grad_in
    ga_ref[...] = grad_in.astype(BF)
    gat_ref[...] = ga_ref[...].T
    for copy in leaving:
        copy.wait()


def backward_call(peers, side, z, gx2, g, x1t, gm, up, down, slope):
    length, width = z.shape
    n = len(up)
    sizes = [len(pieces) for pieces in up]
    inner = up[0][0].shape[1]
    shape = blocks_shape(peers, width, inner)
    outs = [(shape, BF)] * n + [
        ((length, width), F32),
        ((length, width), BF),
        ((width, length), BF),
        ((8, width), F32),
    ]
    got = call(
        lambda *refs: backward_kernel(n, sizes, *refs),
        outs,
        smem_spec() + vmem_specs(5) + any_specs(2 * sum(sizes) + 1),
        any_specs(n) + vmem_specs(4),
        [
            pltpu.VMEM((length, inner), BF),
            pltpu.VMEM((n, width, inner), BF),
            pltpu.VMEM((n, inner, width), BF),
            pltpu.VMEM((n, length, inner), BF),
            pltpu.VMEM((n, *shape), BF),
            pltpu.SemaphoreType.DMA((2 * sum(sizes) + 2 * n,)),
        ],
        8_000_000_000,
    )(side, z, gx2, g, x1t, gm, *sum(up, []), *sum(down, []), slope)
    return got[:n], got[n:]


def pack_kernel(mix_ref, qkv_ref, out_ref):
    group = mix_ref.shape[0]
    out_ref[:, :group] = mix_ref[...].T
    for c in range(qkv_ref.shape[0]):
        out_ref[:, (c + 1) * group : (c + 2) * group] = qkv_ref[c]


def store_blocks(ref, value, me):
    if len(ref.shape) == 2:
        ref[...] = value[...]
        return
    count, share, _ = ref.shape
    bits = count.bit_length() - 1
    for p in range(count):
        apart = p ^ me
        place = sum(((apart >> i) & 1) << (bits - 1 - i) for i in range(bits))
        ref[place] = value[p * share : (p + 1) * share, :]


def blocks_shape(peers, width, columns):
    share = width // peers
    return (peers, share, columns) if share % 16 == 0 else (width, columns)


def choose(index, count, step, source, store):
    for c in range(count):

        @pl.when(index == c)
        def _(c=c):
            store(source[:, c * step : (c + 1) * step])


def project_kernel(parts, mine_ref, feats_ref, w_ref, *rest):
    outs, full = rest[:parts], rest[parts]
    full[...] = dot(feats_ref[...], w_ref[...])
    step = outs[0].shape[1]
    for k, out in enumerate(outs):

        def store(value, out=out):
            out[...] = value.astype(out.dtype)

        choose(mine_ref[0] ^ k, parts, step, full, store)


def outgoing_kernel(parts, mine_ref, own_ref, near_ref, far_ref, box_ref, table_ref, pick_ref, out_ref, full, low):
    stored, chunk = own_ref.shape
    bins = table_ref.shape[1]
    places = lax.broadcasted_iota(jnp.int32, (stored, bins), 1)
    full[...] = jnp.zeros_like(full)
    spare = low.shape[1] - chunk
    lane = lax.broadcasted_iota(jnp.int32, (stored, spare), 1)
    codes = jnp.zeros((stored, spare), F32)
    for c in range(table_ref.shape[0]):
        corner = box_ref[:, c : c + 1]
        full[...] += dot((corner == places).astype(BF), table_ref[c])
        codes = jnp.where(lane == c, corner.astype(F32) + 1.0, codes)
    low[:, chunk:] = codes.astype(BF)

    def store(value):
        total = own_ref[...] + near_ref[...].astype(F32) + far_ref[...].astype(F32)
        low[:, :chunk] = (total + value).astype(BF)

    choose(mine_ref[0], parts, chunk, full, store)
    slots = out_ref.shape[0]
    regions = lax.broadcasted_iota(jnp.int32, (slots, stored), 1)
    out_ref[...] = dot((pick_ref[...] == regions).astype(BF), low[...]).astype(BF)


def place_kernel(pick_ref, rows_ref, *outs):
    slots, chunk = outs[0].shape
    places = lax.broadcasted_iota(jnp.int32, (slots * len(outs), rows_ref.shape[0]), 0)
    chosen = (pick_ref[...] == places).astype(BF)
    placed = dot(chosen, rows_ref[:, :chunk]).astype(BF)
    for k, out in enumerate(outs):
        out[...] = placed[k * slots : (k + 1) * slots, :]


def place_feats_kernel(chunk, pick_ref, rows_ref, feats_ref, out_ref, codes_ref):
    places = lax.broadcasted_iota(jnp.int32, (out_ref.shape[0], feats_ref.shape[0]), 0)
    chosen = (pick_ref[...] == places).astype(BF)
    out_ref[...] = dot(chosen, feats_ref[...]).astype(BF)
    last = rows_ref.shape[1] - 128
    first = chunk - last
    codes_ref[...] = dot(chosen, rows_ref[:, last:]).T[first : first + 8, :]


def move_rows_kernel(pick_ref, rows_ref, out_ref):
    shape = (out_ref.shape[0], rows_ref.shape[0])
    places = lax.broadcasted_iota(jnp.int32, shape, 0)
    out_ref[...] = dot((pick_ref[...] == places).astype(BF), rows_ref[...])


def take_rows_kernel(pick_ref, rows_ref, out_ref):
    shape = (out_ref.shape[0], rows_ref.shape[0])
    places = lax.broadcasted_iota(jnp.int32, shape, 1)
    out_ref[...] = dot((pick_ref[...] == places).astype(BF), rows_ref[...]).astype(BF)


def embed_kernel(parts, mine_ref, text_ref, type_ref, pos_ref, gain_ref, bias_ref, *rest):
    pieces, (emb_ref, hid_ref, x_ref, xt_ref) = rest[:parts], rest[parts:]
    text_len = text_ref.shape[0]
    chunk = pieces[0].shape[1]
    types = type_ref[...].astype(F32)
    pos = pos_ref[...].astype(F32)
    emb_ref[:text_len, :] = text_ref[...].astype(F32) + types[0:1, :] + pos[:text_len, :]
    for k, piece in enumerate(pieces):
        for c in range(parts):

            @pl.when(mine_ref[0] ^ k == c)
            def _(piece=piece, c=c):
                at = slice(c * chunk, (c + 1) * chunk)
                emb_ref[text_len:, at] = piece[...].astype(F32)

    emb_ref[text_len:, :] += types[1:2, :] + pos[text_len:, :]
    hidden, _, _ = layer_norm(emb_ref[...], gain_ref[...], bias_ref[...])
    hid_ref[...] = hidden
    x_ref[...] = hidden.astype(BF)
    xt_ref[...] = x_ref[...].T


def embed_back_kernel(grad_ref, emb_ref, gain_ref, mid_ref, fin_ref, text_ref, reg_ref, vec):
    text_len = text_ref.shape[0]
    slots = emb_ref.shape[0] - text_len
    grad_in, gain_sum, bias_sum = norm_back(grad_ref[...], emb_ref[...], gain_ref[...])
    text_ref[...] = grad_in[:text_len, :].astype(BF)
    reg_ref[:slots, :] = grad_in[text_len:, :].astype(BF)
    vec[...] = jnp.zeros_like(vec)
    vec[0:1, :] = jnp.sum(grad_in[:text_len, :], axis=0, keepdims=True)
    vec[1:2, :] = jnp.sum(grad_in[text_len:, :], axis=0, keepdims=True)
    vec[2:3, :] = gain_sum
    vec[3:4, :] = bias_sum
    vec[4:6, :] = mid_ref[0:2, :]
    vec[6:8, :] = fin_ref[0:2, :]
    reg_ref[slots:, :] = vec[...].astype(BF)


def return_kernel(parts, mine_ref, pick_ref, feats_ref, codes_ref, w_ref, *rest):
    pieces = rest[:parts]
    wire_ref, proj_ref, box_ref, rest_ref, rows, columns, sums, full_ref = rest[parts:]
    slots = rows.shape[0] // parts
    chunk = columns.shape[1]
    for k in range(parts):
        rows[k * slots : (k + 1) * slots, :] = pieces[k][:slots, :]
    low = dot_nt(rows[...], w_ref[...]).astype(BF)
    places = lax.broadcasted_iota(jnp.int32, (wire_ref.shape[0], rows.shape[0]), 1)
    wire_ref[...] = dot((pick_ref[...] == places).astype(BF), low).astype(BF)
    full_ref[...] = dot(rows[...].T, feats_ref[...]).astype(BF)
    store_blocks(proj_ref, full_ref, mine_ref[1])
    sums[...] = pieces[0][...].astype(F32)
    for k in range(1, parts):
        sums[...] += pieces[k][...].astype(F32)

    def store_rows(value):
        columns[...] = value

    def store_rest(value):
        rest_ref[...] = value

    choose(mine_ref[0], parts, chunk, rows, store_rows)
    choose(mine_ref[0], parts, chunk, sums, store_rest)
    bins = box_ref.shape[1]
    codes = lax.broadcasted_iota(jnp.int32, (bins, rows.shape[0]), 0).astype(F32) + 1.0
    for c in range(box_ref.shape[0]):
        box_ref[c] = dot((codes_ref[c : c + 1, :] == codes).astype(BF), columns[...])


def text_kernel(parts, mine_ref, *rest):
    pieces, (out_ref, pos_ref, sums) = rest[:parts], rest[parts:]
    sums[...] = pieces[0][...].astype(F32)
    out_ref[mine_ref[0]] = sums[...]
    for k in range(1, parts):
        value = pieces[k][...].astype(F32)
        out_ref[mine_ref[0] ^ k] = value
        sums[...] += value

    def store(value):
        pos_ref[...] = value

    choose(mine_ref[0], parts, pos_ref.shape[1], sums, store)


def line_up_kernel(parts, mine_ref, *rest):
    pieces, out_ref = rest[:parts], rest[parts]
    for k in range(parts):
        out_ref[mine_ref[0] ^ k] = pieces[k][...]


def spread_kernel(parts, chunks_ref, out_ref):
    chunk = chunks_ref.shape[2]
    for c in range(parts):
        out_ref[:, c * chunk : (c + 1) * chunk] = chunks_ref[c]


def small_call(body, args, outs, scratch=(), scalar=False):
    specs = vmem_specs(len(args))
    if scalar:
        specs[0] = pl.BlockSpec(memory_space=pltpu.SMEM)
    got = call(body, outs, specs, vmem_specs(len(outs)), list(scratch), 1 << 20, 1 << 16)(*args)
    return got[0] if len(outs) == 1 else got


def swap(value, axis, bit):
    count = lax.axis_size(axis)
    return lax.ppermute(value, axis, [(i, i ^ bit) for i in range(count)])


def bits_of(axis):
    count = lax.axis_size(axis)
    return [1 << i for i in range(count.bit_length() - 1)]


def tie(first, second):
    return lax.optimization_barrier((first, second))


def after(value, first):
    return lax.optimization_barrier((value, first))[0]


def far_half(shard, bit):
    rows = shard.shape[0] // 2
    side = (lax.axis_index("dp") // bit) % 2
    return swap(lax.dynamic_slice_in_dim(shard, side * rows, rows, 0), "tensor", 2)


def gather_shards(shard, half, other):
    return [
        [shard],
        [swap(shard, "tensor", 1)],
        [half, other],
        [swap(half, "tensor", 1), swap(other, "tensor", 1)],
    ]


def pair_sum(terms):
    here = [terms[0], swap(terms[1], "tensor", 1)]
    return here, total([terms[2], swap(terms[3], "tensor", 1)]).astype(BF)


def total(summands):
    return sum(value.astype(F32) for value in summands)


def hop(values, bit):
    if values[0].ndim == 2:
        return values, None
    half = values[0].shape[0] // 2
    sent = total([v[half:] for v in values]).astype(BF)
    return [v[:half] for v in values], swap(sent, "dp", bit)


def finish(values, bits):
    if values[0].ndim == 2:
        term = total([v for v in values if v is not None]).astype(BF)
        term = term.reshape(lax.axis_size("dp"), -1, term.shape[1])
        return jnp.sum(lax.all_to_all(term, "dp", 0, 0, tiled=True).astype(F32), axis=0)
    for bit in bits:
        stay, come = hop(values, bit)
        values = stay + [come]
    return total(values)[0]


def local(
    text_embed,
    region_feats,
    box_coords,
    seg_ids,
    region_counts,
    send_index,
    recv_pos,
    w_proj,
    box_table,
    type_embed,
    pos_embed,
    gain_embed,
    bias_embed,
    w_qkv,
    w_mix,
    gain_mid,
    bias_mid,
    w_up,
    w_down,
    gain_final,
    bias_final,
    cotangent,
):
    parts = lax.axis_size("tensor")
    peers = lax.axis_size("dp")
    mine = lax.axis_index("tensor")
    dp_now = lax.axis_index("dp")
    mine_now = jnp.stack([mine, dp_now]).astype(jnp.int32)
    sides = jnp.stack([dp_now % 2, dp_now % 2, (dp_now // 2) % 2, dp_now]).astype(jnp.int32)
    row_count, text_len, width = text_embed.shape
    assert row_count == parts == 4
    length = seg_ids.shape[1]
    slots = length - text_len
    stored, depth = region_feats.shape
    capacity = send_index.shape[2]
    bins = box_table.shape[1]
    group = w_qkv.shape[2]
    heads = group // HD
    chunk = width // parts
    share = width // peers
    broad = -(-(chunk + 8) // 128) * 128
    wire = peers * capacity

    def own(array):
        return lax.dynamic_index_in_dim(array, mine, 0, keepdims=False)

    def line(vector):
        return vector.reshape(1, width)

    held = small_call(
        lambda *refs: project_kernel(parts, *refs),
        [mine_now, region_feats, w_proj],
        [((stored, chunk), F32 if k == 0 else BF) for k in range(parts)],
        [pltpu.VMEM((stored, width), F32)],
        scalar=True,
    )
    near = swap(held[1], "tensor", 1)
    across = (held[2].astype(F32) + swap(held[3], "tensor", 1).astype(F32)).astype(BF)

    across, (w_mix, w_qkv) = tie(across, (w_mix, w_qkv))
    far = swap(across, "tensor", 2)
    packed = small_call(pack_kernel, [w_mix, w_qkv], [((width, width), BF)])
    far, packed = tie(far, packed)
    att_half = far_half(packed, 1)

    send_flat = send_index.reshape(-1)
    recv_flat = recv_pos.reshape(-1)
    recv_slot = jnp.where(
        recv_flat >= 0,
        (recv_flat // length) * slots + recv_flat % length - text_len,
        -1,
    )
    recv_near = jnp.where(recv_flat >= 0, (recv_slot // slots ^ mine) * slots + recv_slot % slots, -1)
    near_line, near_column = recv_near.reshape(1, wire), recv_near.reshape(wire, 1)
    send_line, send_column = send_flat.reshape(1, wire), send_flat.reshape(wire, 1)
    outgoing = small_call(
        lambda *refs: outgoing_kernel(parts, *refs),
        [mine_now, held[0], near, far, box_coords, box_table, send_column],
        [((wire, broad), BF)],
        [pltpu.VMEM((stored, width), F32), pltpu.VMEM((stored, broad), BF)],
        scalar=True,
    )
    outgoing, w_up = tie(outgoing, w_up)
    up_half = far_half(w_up, 1)
    incoming = lax.all_to_all(
        outgoing.reshape(peers, capacity, broad), "dp", 0, 0, tiled=True
    ).reshape(wire, broad)
    allowed = key_mask(own(seg_ids), own(region_counts))
    incoming, (att_half, allow, allow_turned, text_mine) = tie(
        incoming, (att_half, allowed.astype(F32), allowed.T.astype(F32), own(text_embed))
    )
    att_other = swap(att_half, "dp", 1)
    placed = small_call(
        place_kernel, [near_line, incoming], [((slots, chunk), BF)] * row_count
    )
    placed = [swap(piece, "tensor", k) if k else piece for k, piece in enumerate(placed)]
    placed, w_down = tie(placed, w_down)
    down_half = far_half(w_down, 2)

    embedded, hidden0, inputs0, inputs0_turned = small_call(
        lambda *refs: embed_kernel(parts, *refs),
        [mine_now, text_mine, type_embed, pos_embed, line(gain_embed), line(bias_embed)] + placed,
        [
            ((length, width), F32),
            ((length, width), F32),
            ((length, width), BF),
            ((width, length), BF),
        ],
        scalar=True,
    )
    (hidden0, inputs0), feats = tie((hidden0, inputs0), region_feats)
    feats_wire = small_call(take_rows_kernel, [send_column, feats], [((wire, depth), BF)])
    feats_wire = lax.all_to_all(
        feats_wire.reshape(peers, capacity, depth), "dp", 0, 0, tiled=True
    ).reshape(wire, depth)
    (hidden0, inputs0), (up_half, att_other) = tie((hidden0, inputs0), (up_half, att_other))
    up_other = swap(up_half, "dp", 1)
    att_shards = gather_shards(packed, att_half, att_other)
    z, near_helds, near_lses = attend_call(heads, sides, inputs0, hidden0, allow, att_shards[:2])
    z, (up_other, down_half) = tie(z, (up_other, down_half))
    down_other = swap(down_half, "dp", 2)
    up = gather_shards(w_up, up_half, up_other)
    z, far_helds, far_lses = attend_call(heads, sides, inputs0, z, allow, att_shards[2:])
    helds, lses = near_helds + far_helds, near_lses + far_lses
    z, down_other = tie(z, down_other)
    down = gather_shards(w_down, down_half, down_other)
    slopes, down_terms, (final, x1t, grad_x2, grad_ffn, final_vectors) = forward_call(
        peers,
        sides,
        z,
        own(cotangent),
        line(gain_mid),
        line(bias_mid),
        line(gain_final),
        line(bias_final),
        up,
        down,
    )
    down_here, down_across = pair_sum(down_terms)
    final_far = swap(final, "tensor", 2)

    up_terms, (grad_x1, grad_attn, grad_attn_turned, mid_vectors) = backward_call(
        peers, sides, z, grad_x2, grad_ffn, x1t, line(gain_mid), up, down, slopes
    )
    (grad_attn, grad_x1), (down_across, final_far, feats_wire) = tie(
        (grad_attn, grad_x1), (down_across, final_far, feats_wire)
    )
    down_far = swap(down_across, "tensor", 2)
    up_here, up_across = pair_sum(up_terms)
    slot_feats, slot_codes = small_call(
        lambda *refs: place_feats_kernel(chunk, *refs),
        [near_line, incoming, feats_wire],
        [((row_count * slots, depth), BF), ((8, row_count * slots), F32)],
    )
    total0 = grad_x1
    att_terms = [None] * parts
    for at in (1, 0):
        picked = range(at, parts, 2)
        total0, terms = attend_back_call(
            heads,
            peers,
            sides,
            grad_attn,
            grad_attn_turned,
            inputs0_turned,
            total0,
            allow_turned,
            [att_shards[k] for k in picked],
            [helds[k] for k in picked],
            [lses[k] for k in picked],
        )
        for k, term in zip(picked, terms, strict=True):
            att_terms[k] = term
        if at:
            total0, (up_across, slot_feats) = tie(total0, (up_across, slot_feats))
            up_far = swap(up_across, "tensor", 2)
    total0, down_far = tie(total0, down_far)
    att_here, att_across = pair_sum(att_terms)

    def neighbours(piece, far):
        return [piece, swap(piece, "tensor", 1), far, swap(far, "tensor", 1)]

    text_own, regions_own = small_call(
        embed_back_kernel,
        [total0, embedded, line(gain_embed), mid_vectors, final_vectors],
        [((text_len, width), BF), ((slots + 16, width), BF)],
        [pltpu.VMEM((16, width), F32)],
    )
    regions_far = swap(regions_own, "tensor", 2)
    first_bit, *rest_bits = bits_of("dp")
    down_stay, down_come = hop(down_here + [down_far], first_bit)
    up_stay, up_come = hop(up_here + [up_far], first_bit)
    text_far = swap(after(text_own, regions_far), "tensor", 2)
    feats_back, proj_term, box_term, rest_sum = small_call(
        lambda *refs: return_kernel(parts, *refs),
        [mine_now, near_column, slot_feats, slot_codes, w_proj]
        + neighbours(regions_own, regions_far),
        [
            ((wire, depth), BF),
            (blocks_shape(peers, width, depth), BF),
            ((box_table.shape[0], bins, chunk), F32),
            ((slots + 16, chunk), F32),
        ],
        [
            pltpu.VMEM((row_count * slots, width), BF),
            pltpu.VMEM((row_count * slots, chunk), BF),
            pltpu.VMEM((slots + 16, width), F32),
            pltpu.VMEM((width, depth), BF),
        ],
        scalar=True,
    )
    att_far = swap(after(att_across, proj_term), "tensor", 2)
    proj_stay, proj_come = hop([proj_term], first_bit)
    feats_back = lax.all_to_all(
        feats_back.reshape(peers, capacity, depth), "dp", 0, 0, tiled=True
    ).reshape(wire, depth)
    feat_grad = small_call(move_rows_kernel, [send_line, feats_back], [((stored, depth), F32)])
    text_grad, text_sum = small_call(
        lambda *refs: text_kernel(parts, *refs),
        [mine_now] + neighbours(text_own, text_far),
        [((parts, text_len, width), F32), ((text_len, chunk), F32)],
        [pltpu.VMEM((text_len, width), F32)],
        scalar=True,
    )
    pos_term = jnp.concatenate([text_sum, rest_sum[:slots]], axis=0)
    bin_share = bins // peers
    pos_share = length // peers
    bundle = jnp.concatenate(
        [
            pos_term.reshape(peers, pos_share, chunk),
            box_term.reshape(-1, peers, bin_share, chunk)
            .transpose(1, 0, 2, 3)
            .reshape(peers, -1, chunk),
            jnp.broadcast_to(rest_sum[slots:], (peers, 16, chunk)),
        ],
        axis=1,
    ).astype(BF)
    grad_down = finish(down_stay + [down_come], rest_bits).T
    grad_up = finish(up_stay + [up_come], rest_bits)
    if proj_come is not None:
        proj_come = after(proj_come, text_sum)
    grad_proj = finish(proj_stay + [proj_come], rest_bits).T
    att_stay, att_come = hop(att_here + [att_far], first_bit)
    layer_output = small_call(
        lambda *refs: line_up_kernel(parts, *refs),
        [mine_now] + neighbours(final, after(final_far, bundle)),
        [((parts, length, width), BF)],
        scalar=True,
    )
    if att_come is not None:
        att_come = after(att_come, (layer_output, feat_grad))
    grad_att = finish(att_stay + [att_come], rest_bits)
    bundle = jnp.sum(
        lax.all_to_all(bundle, "dp", 0, 0, tiled=True).astype(F32), axis=0
    )
    bundle = lax.all_gather(bundle, "tensor", axis=0, tiled=False)
    bundle = small_call(
        lambda *refs: spread_kernel(parts, *refs), [bundle], [((bundle.shape[1], width), F32)]
    )
    grad_pos = bundle[:pos_share]
    grad_box = bundle[pos_share:-16].reshape(-1, bin_share, width)
    vectors = lax.dynamic_slice_in_dim(bundle[-16:], lax.axis_index("dp") * share, share, 1)

    grad_mix = grad_att[:, :group].T
    grad_qkv = grad_att[:, group:].reshape(share, 3, group).transpose(1, 0, 2)
    return (
        layer_output,
        text_grad,
        feat_grad,
        grad_proj,
        grad_box,
        vectors[:2],
        grad_pos,
        vectors[2],
        vectors[3],
        grad_qkv,
        grad_mix,
        vectors[4],
        vectors[5],
        grad_up,
        grad_down,
        vectors[6],
        vectors[7],
    )


def solution(mesh):
    return jax.shard_map(
        local,
        mesh=mesh,
        in_specs=(
            P("dp", None, None),
            P("dp", "tensor"),
            P("dp", None),
            P("dp", None),
            P("dp"),
            P("dp", None, None),
            P("dp", None, None),
            P("tensor", None),
            P(),
            P(),
            P(),
            P(),
            P(),
            P(None, None, "tensor"),
            P("tensor", None),
            P(),
            P(),
            P(None, "tensor"),
            P("tensor", None),
            P(),
            P(),
            P("dp", None, None),
        ),
        out_specs=(
            P("dp", None, None),
            P("dp", None, None),
            P("dp", "tensor"),
            P("tensor", "dp"),
            P(None, "dp", None),
            P(None, "dp"),
            P("dp", None),
            P("dp"),
            P("dp"),
            P(None, "dp", "tensor"),
            P("tensor", "dp"),
            P("dp"),
            P("dp"),
            P("dp", "tensor"),
            P("tensor", "dp"),
            P("dp"),
            P("dp"),
        ),
        check_vma=False,
    )
```

```python
import jax
import jax.numpy as jnp
from jax import lax
from jax.experimental import pallas as pl
from jax.experimental.pallas import tpu as pltpu
from jax.sharding import PartitionSpec as P

HD = 64
LT = 384
EPSILON = 1e-06
NEGATIVE = -1000000000.0
BF = jnp.bfloat16
F32 = jnp.float32


def layer_norm(values, gain, bias):
    mean = jnp.mean(values, axis=-1, keepdims=True)
    centred = values - mean
    variance = jnp.mean(centred * centred, axis=-1, keepdims=True)
    inverse = lax.rsqrt(variance + EPSILON)
    normed = centred * inverse
    return (normed * gain + bias, normed, inverse)


def key_mask(seg_row, count):
    length = seg_row.shape[0]
    places = jnp.arange(length, dtype=jnp.int32)
    usable = places < LT + count
    same = seg_row[:, None] == seg_row[None, :]
    return same & (usable[None, :] | (places[:, None] == places[None, :]))


VMEM_BYTES = 52 << 20
ROOT_HALF = 0.7071067811865476
DENSITY = 0.3989422804014327


def dot(a, b):
    return jnp.dot(a, b, preferred_element_type=F32)


def dot_nt(a, b):
    return lax.dot_general(a, b, (((1,), (1,)), ((), ())), preferred_element_type=F32)


def dot_tn(a, b):
    return lax.dot_general(a, b, (((0,), (0,)), ((), ())), preferred_element_type=F32)


def any_specs(count):
    return [pl.BlockSpec(memory_space=pl.ANY)] * count


def smem_spec():
    return [pl.BlockSpec(memory_space=pltpu.SMEM)]


def vmem_specs(count):
    return [pl.BlockSpec(memory_space=pltpu.VMEM)] * count


def call(body, outs, in_specs, out_specs, scratch, flops, moved=16 << 20):
    return pl.pallas_call(
        body,
        out_shape=[jax.ShapeDtypeStruct(shape, kind) for shape, kind in outs],
        in_specs=in_specs,
        out_specs=out_specs,
        scratch_shapes=scratch,
        compiler_params=pltpu.CompilerParams(vmem_limit_bytes=VMEM_BYTES),
        cost_estimate=pl.CostEstimate(flops=flops, bytes_accessed=moved, transcendentals=0),
    )


def attend_kernel(heads, sizes, side_ref, x_ref, z_ref, allow_ref, *rest):
    count = len(sizes)
    shards, rest = regroup(rest, sizes)
    zout_ref, helds, lses = rest[0], rest[1 : 1 + count], rest[1 + count : 1 + 2 * count]
    weights, sems = rest[1 + 2 * count :]
    started, _ = fetch_shards(shards, weights, side_ref[0], sems)
    length, width = x_ref.shape
    group = heads * HD
    block = length
    lane = lax.broadcasted_iota(jnp.int32, (block, 128), 1)
    for i in range(count):
        for copy in started[i]:
            copy.wait()
        w_ref, held, lse_ref = weights.at[i], helds[i], lses[i]
        mixed = dot(x_ref[...], w_ref[...])
        held[:, group : 2 * group] = (mixed[:, group : 2 * group] * HD ** (-0.5)).astype(BF)
        held[:, 2 * group :] = mixed[:, 2 * group :].astype(BF)

        def rows(b, carry):
            at = pl.ds(pl.multiple_of(b * block, block), block)
            columns = jnp.zeros((block, 128), F32)
            allow = allow_ref[at, :] > 0.5
            for h in range(heads):
                q = held[at, group + h * HD : group + (h + 1) * HD]
                k = held[:, 2 * group + h * HD : 2 * group + (h + 1) * HD]
                v = held[:, 3 * group + h * HD : 3 * group + (h + 1) * HD]
                scores = jnp.where(allow, dot_nt(q, k), NEGATIVE)
                top = jnp.max(scores, axis=1, keepdims=True)
                raised = jnp.exp(scores - top)
                total = jnp.sum(raised, axis=1, keepdims=True)
                context = dot(raised.astype(BF), v) / total
                held[at, h * HD : (h + 1) * HD] = context.astype(BF)
                columns = jnp.where(lane == h, top + jnp.log(total), columns)
            lse_ref[:, at] = columns.T[:8, :]
            return carry

        for b in range(length // block):
            rows(b, 0)
        if i == 0:
            zout_ref[...] = z_ref[...] + dot_nt(held[:, :group], w_ref[:, :group])
        else:
            zout_ref[...] += dot_nt(held[:, :group], w_ref[:, :group])


def attend_call(heads, side, x, z, allow, shards):
    length, width = x.shape
    n = len(shards)
    sizes = [len(pieces) for pieces in shards]
    outs = [((length, width), F32)] + [((length, width), BF)] * n + [((8, length), F32)] * n
    got = call(
        lambda *refs: attend_kernel(heads, sizes, *refs),
        outs,
        smem_spec() + vmem_specs(3) + any_specs(sum(sizes)),
        vmem_specs(len(outs)),
        [pltpu.VMEM((n, width, width), BF), pltpu.SemaphoreType.DMA((sum(sizes),))],
        n * 2_000_000_000,
    )(side, x, z, allow, *sum(shards, []))
    return got[0], got[1 : 1 + n], got[1 + n :]


def attend_back_kernel(heads, sizes, side_ref, g_ref, gt_ref, xt_ref, acc_ref, allow_ref, *rest):
    count = len(sizes)
    shards, rest = regroup(rest, sizes)
    helds, lses = rest[:count], rest[count : 2 * count]
    accout_ref, terms = rest[2 * count], rest[2 * count + 1 : 3 * count + 1]
    gc_ref, grads, dq_ref, delta_ref, weights, full_ref, sems = rest[3 * count + 1 :]
    started, _ = fetch_shards(shards, weights, side_ref[0], sems)
    length, width = g_ref.shape
    group = heads * HD
    block = length
    lane = lax.broadcasted_iota(jnp.int32, (length, 128), 1)
    for i in range(count):
        for copy in started[i]:
            copy.wait()
        w_ref, held, lse_ref = weights.at[i], helds[i], lses[i]
        low = dot(g_ref[...], w_ref[:, :group]).astype(BF)
        gc_ref[...] = low
        product = low.astype(F32) * held[:, :group].astype(F32)
        columns = jnp.zeros((length, 128), F32)
        for h in range(heads):
            inner = jnp.sum(product[:, h * HD : (h + 1) * HD], axis=1, keepdims=True)
            columns = jnp.where(lane == h, inner, columns)
        delta_ref[...] = columns.T[:8, :]
        dq_ref[...] = jnp.zeros_like(dq_ref)
        grads[:, :group] = jnp.zeros((length, group), BF)

        def rows(b, carry):
            at = pl.ds(pl.multiple_of(b * block, block), block)
            allow = allow_ref[at, :] > 0.5
            for h in range(heads):
                q = held[:, group + h * HD : group + (h + 1) * HD]
                k = held[at, 2 * group + h * HD : 2 * group + (h + 1) * HD]
                v = held[at, 3 * group + h * HD : 3 * group + (h + 1) * HD]
                gc = gc_ref[:, h * HD : (h + 1) * HD]
                scores = jnp.where(allow, dot_nt(k, q), NEGATIVE)
                probs = jnp.exp(scores - lse_ref[h : h + 1, :])
                grad_probs = dot_nt(v, gc)
                grad_scores = (probs * (grad_probs - delta_ref[h : h + 1, :])).astype(BF)
                grads[at, 3 * group + h * HD : 3 * group + (h + 1) * HD] = dot(
                    probs.astype(BF), gc
                ).astype(BF)
                grads[at, 2 * group + h * HD : 2 * group + (h + 1) * HD] = dot(
                    grad_scores, q
                ).astype(BF)
                dq_ref[h * HD : (h + 1) * HD, :] += dot_tn(k, grad_scores)
            return carry

        for b in range(length // block):
            rows(b, 0)
        grads[:, group : 2 * group] = (dq_ref[...] * HD ** (-0.5)).T.astype(BF)
        if i == 0:
            accout_ref[...] = acc_ref[...] + dot_nt(grads[...], w_ref[...])
        else:
            accout_ref[...] += dot_nt(grads[...], w_ref[...])
        full_ref[...] = dot(xt_ref[...], grads[...]).astype(BF)
        full_ref[:, :group] = dot(gt_ref[...], held[:, :group]).astype(BF)
        store_blocks(terms[i], full_ref, side_ref[3])


def attend_back_call(heads, peers, side, g, gt, xt, acc, allow, shards, helds, lses):
    length, width = g.shape
    n = len(shards)
    sizes = [len(pieces) for pieces in shards]
    group = heads * HD
    outs = [((length, width), F32)] + [(blocks_shape(peers, width, width), BF)] * n
    got = call(
        lambda *refs: attend_back_kernel(heads, sizes, *refs),
        outs,
        smem_spec() + vmem_specs(5) + any_specs(sum(sizes)) + vmem_specs(2 * n),
        vmem_specs(len(outs)),
        [
            pltpu.VMEM((length, group), BF),
            pltpu.VMEM((length, width), BF),
            pltpu.VMEM((group, length), F32),
            pltpu.VMEM((8, length), F32),
            pltpu.VMEM((n, width, width), BF),
            pltpu.VMEM((width, width), BF),
            pltpu.SemaphoreType.DMA((sum(sizes),)),
        ],
        n * 4_000_000_000,
    )(side, g, gt, xt, acc, allow, *sum(shards, []), *helds, *lses)
    return got[0], got[1:]


def erf(x):
    x = jnp.clip(x, -4.0, 4.0)
    s = x * x
    top = jnp.full_like(x, -2.72614225801306e-10)
    for c in (
        2.77068142495902e-08,
        -2.10102402082508e-06,
        -5.69250639462346e-05,
        -7.34990630326855e-04,
        -2.95459980854025e-03,
        -1.60960333262415e-02,
    ):
        top = top * s + c
    base = jnp.full_like(x, -1.45660718464996e-05)
    for c in (
        -2.13374055278905e-04,
        -1.68282697438203e-03,
        -7.37332916720468e-03,
        -1.42647390514189e-02,
    ):
        base = base * s + c
    return x * top / base


def norm_back(grad, values, gain):
    _, normed, inverse = layer_norm(values, gain, 0.0)
    scaled = grad * gain
    mean_grad = jnp.mean(scaled, axis=-1, keepdims=True)
    mean_proj = jnp.mean(scaled * normed, axis=-1, keepdims=True)
    return (
        inverse * (scaled - mean_grad - normed * mean_proj),
        jnp.sum(grad * normed, axis=0, keepdims=True),
        jnp.sum(grad, axis=0, keepdims=True),
    )


def regroup(flat, sizes):
    flat = list(flat)
    return [[flat.pop(0) for _ in range(size)] for size in sizes], flat


def fetch_shards(shards, target, side, sems, base=0):
    started = []
    for i, pieces in enumerate(shards):
        copies = []
        for j, piece in enumerate(pieces):
            rows = piece.shape[0]
            at = pl.ds(pl.multiple_of((side if j == 0 else 1 - side) * rows, 16), rows)
            place = target.at[i] if len(pieces) == 1 else target.at[i, at]
            copies.append(pltpu.make_async_copy(piece, place, sems.at[base]))
            copies[-1].start()
            base += 1
        started.append(copies)
    return started, base


def forward_kernel(
    parts, sizes, side_ref, z_ref, cot_ref, gm_ref, bm_ref, gf_ref, bf_ref, *rest
):
    up_shards, rest = regroup(rest, sizes)
    down_shards, rest = regroup(rest, sizes)
    slope_any, terms = rest[0], rest[1 : parts + 1]
    out_ref, x1t_ref, gx2_ref, g_ref, vec_ref = rest[parts + 1 : parts + 6]
    ups, downs, actives, ffn_ref, x1_ref, gt_ref, slope_ref, held, sems = rest[parts + 6 :]
    up_started, down_started, base = [], [], 0
    for k in range(parts):
        copies, base = fetch_shards([up_shards[k]], ups.at[k : k + 1], side_ref[1], sems, base)
        up_started += copies
        copies, base = fetch_shards([down_shards[k]], downs.at[k : k + 1], side_ref[2], sems, base)
        down_started += copies
    leaving = []

    def leave(source, target):
        leaving.append(pltpu.make_async_copy(source, target, sems.at[base + len(leaving)]))
        leaving[-1].start()

    length, width = z_ref.shape
    block = 256
    vec_ref[...] = jnp.zeros_like(vec_ref)
    for b in range(length // block):
        at = slice(b * block, (b + 1) * block)
        hidden1, _, _ = layer_norm(z_ref[at, :], gm_ref[...], bm_ref[...])
        x1_ref[at, :] = hidden1.astype(BF)
        ffn_ref[at, :] = hidden1
        for k in range(parts):
            if b == 0:
                for copy in up_started[k]:
                    copy.wait()
            before = dot(x1_ref[at, :], ups[k])
            half = 0.5 + 0.5 * erf(before * ROOT_HALF)
            slope_ref[k, at, :] = (
                half + before * (DENSITY * jnp.exp(-0.5 * before * before))
            ).astype(BF)
            actives[k, at, :] = (before * half).astype(BF)
            if b == 0:
                for copy in down_started[k]:
                    copy.wait()
            ffn_ref[at, :] += dot(actives[k, at, :], downs[k])
            if at.stop == length:
                leave(slope_ref.at[k], slope_any.at[k])
        final, normed, inverse = layer_norm(ffn_ref[at, :], gf_ref[...], bf_ref[...])
        out_ref[at, :] = final.astype(BF)
        grad_in, gain_sum, bias_sum = norm_back(
            cot_ref[at, :].astype(F32), ffn_ref[at, :], gf_ref[...]
        )
        vec_ref[0:1, :] += gain_sum
        vec_ref[1:2, :] += bias_sum
        gx2_ref[at, :] = grad_in
        g_ref[at, :] = grad_in.astype(BF)
    gt_ref[...] = g_ref[...].T
    for k in sorted(range(parts), key=lambda k: (1 - k % 2, k)):
        store_blocks(held.at[k], dot(gt_ref[...], actives[k]).astype(BF), side_ref[3])
        leave(held.at[k], terms[k])
    x1t_ref[...] = x1_ref[...].T
    for copy in leaving:
        copy.wait()


def forward_call(peers, side, z, cot, gm, bm, gf, bf, up, down):
    length, width = z.shape
    n = len(up)
    sizes = [len(pieces) for pieces in up]
    inner = up[0][0].shape[1]
    shape = blocks_shape(peers, width, inner)
    outs = (
        [((n, length, inner), BF)]
        + [(shape, BF)] * n
        + [
            ((length, width), BF),
            ((width, length), BF),
            ((length, width), F32),
            ((length, width), BF),
            ((8, width), F32),
        ]
    )
    got = call(
        lambda *refs: forward_kernel(n, sizes, *refs),
        outs,
        smem_spec() + vmem_specs(6) + any_specs(2 * sum(sizes)),
        any_specs(n + 1) + vmem_specs(5),
        [
            pltpu.VMEM((n, width, inner), BF),
            pltpu.VMEM((n, inner, width), BF),
            pltpu.VMEM((n, length, inner), BF),
            pltpu.VMEM((length, width), F32),
            pltpu.VMEM((length, width), BF),
            pltpu.VMEM((width, length), BF),
            pltpu.VMEM((n, length, inner), BF),
            pltpu.VMEM((n, *shape), BF),
            pltpu.SemaphoreType.DMA((2 * sum(sizes) + 2 * n,)),
        ],
        8_000_000_000,
    )(side, z, cot, gm, bm, gf, bf, *sum(up, []), *sum(down, []))
    return got[0], got[1 : n + 1], got[n + 1 :]


def backward_kernel(
    parts, sizes, side_ref, z_ref, gx2_ref, g_ref, x1t_ref, gm_ref, *rest
):
    up_shards, rest = regroup(rest, sizes)
    down_shards, rest = regroup(rest, sizes)
    slope_any, *rest = rest
    terms = rest[:parts]
    gx1_ref, ga_ref, gat_ref, vec_ref, gb_ref, ups, downs, slopes, held, sems = rest[parts:]
    order = sorted(range(parts), key=lambda k: (1 - k % 2, k))
    started, base = {}, 0
    for k in order:
        first, base = fetch_shards([down_shards[k]], downs.at[k : k + 1], side_ref[2], sems, base)
        slope = pltpu.make_async_copy(slope_any.at[k], slopes.at[k], sems.at[base])
        slope.start()
        second, base = fetch_shards([up_shards[k]], ups.at[k : k + 1], side_ref[1], sems, base + 1)
        started[k] = first[0] + [slope], second[0]
    leaving = []
    gx1_ref[...] = gx2_ref[...]
    for k in order:
        for copy in started[k][0]:
            copy.wait()
        gb_ref[...] = (dot_nt(g_ref[...], downs[k]) * slopes[k].astype(F32)).astype(BF)
        store_blocks(held.at[k], dot(x1t_ref[...], gb_ref[...]).astype(BF), side_ref[3])
        leaving.append(pltpu.make_async_copy(held.at[k], terms[k], sems.at[base + len(leaving)]))
        leaving[-1].start()
        for copy in started[k][1]:
            copy.wait()
        gx1_ref[...] += dot_nt(gb_ref[...], ups[k])
    grad_in, gain_sum, bias_sum = norm_back(gx1_ref[...], z_ref[...], gm_ref[...])
    vec_ref[...] = jnp.zeros_like(vec_ref)
    vec_ref[0:1, :] = gain_sum
    vec_ref[1:2, :] = bias_sum
    gx1_ref[...] = grad_in
    ga_ref[...] = grad_in.astype(BF)
    gat_ref[...] = ga_ref[...].T
    for copy in leaving:
        copy.wait()


def backward_call(peers, side, z, gx2, g, x1t, gm, up, down, slope):
    length, width = z.shape
    n = len(up)
    sizes = [len(pieces) for pieces in up]
    inner = up[0][0].shape[1]
    shape = blocks_shape(peers, width, inner)
    outs = [(shape, BF)] * n + [
        ((length, width), F32),
        ((length, width), BF),
        ((width, length), BF),
        ((8, width), F32),
    ]
    got = call(
        lambda *refs: backward_kernel(n, sizes, *refs),
        outs,
        smem_spec() + vmem_specs(5) + any_specs(2 * sum(sizes) + 1),
        any_specs(n) + vmem_specs(4),
        [
            pltpu.VMEM((length, inner), BF),
            pltpu.VMEM((n, width, inner), BF),
            pltpu.VMEM((n, inner, width), BF),
            pltpu.VMEM((n, length, inner), BF),
            pltpu.VMEM((n, *shape), BF),
            pltpu.SemaphoreType.DMA((2 * sum(sizes) + 2 * n,)),
        ],
        8_000_000_000,
    )(side, z, gx2, g, x1t, gm, *sum(up, []), *sum(down, []), slope)
    return got[:n], got[n:]


def pack_kernel(mix_ref, qkv_ref, out_ref):
    group = mix_ref.shape[0]
    out_ref[:, :group] = mix_ref[...].T
    for c in range(qkv_ref.shape[0]):
        out_ref[:, (c + 1) * group : (c + 2) * group] = qkv_ref[c]


def store_blocks(ref, value, me):
    if len(ref.shape) == 2:
        ref[...] = value[...]
        return
    count, share, _ = ref.shape
    bits = count.bit_length() - 1
    for p in range(count):
        apart = p ^ me
        place = sum(((apart >> i) & 1) << (bits - 1 - i) for i in range(bits))
        ref[place] = value[p * share : (p + 1) * share, :]


def blocks_shape(peers, width, columns):
    share = width // peers
    return (peers, share, columns) if share % 16 == 0 else (width, columns)


def choose(index, count, step, source, store):
    for c in range(count):

        @pl.when(index == c)
        def _(c=c):
            store(source[:, c * step : (c + 1) * step])


def project_kernel(parts, mine_ref, feats_ref, w_ref, *rest):
    outs, full = rest[:parts], rest[parts]
    full[...] = dot(feats_ref[...], w_ref[...])
    step = outs[0].shape[1]
    for k, out in enumerate(outs):

        def store(value, out=out):
            out[...] = value.astype(out.dtype)

        choose(mine_ref[0] ^ k, parts, step, full, store)


def outgoing_kernel(parts, mine_ref, own_ref, near_ref, far_ref, box_ref, table_ref, pick_ref, out_ref, full, low):
    stored, chunk = own_ref.shape
    bins = table_ref.shape[1]
    places = lax.broadcasted_iota(jnp.int32, (stored, bins), 1)
    full[...] = jnp.zeros_like(full)
    spare = low.shape[1] - chunk
    lane = lax.broadcasted_iota(jnp.int32, (stored, spare), 1)
    codes = jnp.zeros((stored, spare), F32)
    for c in range(table_ref.shape[0]):
        corner = box_ref[:, c : c + 1]
        full[...] += dot((corner == places).astype(BF), table_ref[c])
        codes = jnp.where(lane == c, corner.astype(F32) + 1.0, codes)
    low[:, chunk:] = codes.astype(BF)

    def store(value):
        total = own_ref[...] + near_ref[...].astype(F32) + far_ref[...].astype(F32)
        low[:, :chunk] = (total + value).astype(BF)

    choose(mine_ref[0], parts, chunk, full, store)
    slots = out_ref.shape[0]
    regions = lax.broadcasted_iota(jnp.int32, (slots, stored), 1)
    out_ref[...] = dot((pick_ref[...] == regions).astype(BF), low[...]).astype(BF)


def place_kernel(pick_ref, rows_ref, *outs):
    slots, chunk = outs[0].shape
    places = lax.broadcasted_iota(jnp.int32, (slots * len(outs), rows_ref.shape[0]), 0)
    chosen = (pick_ref[...] == places).astype(BF)
    placed = dot(chosen, rows_ref[:, :chunk]).astype(BF)
    for k, out in enumerate(outs):
        out[...] = placed[k * slots : (k + 1) * slots, :]


def place_feats_kernel(chunk, pick_ref, rows_ref, feats_ref, out_ref, codes_ref):
    places = lax.broadcasted_iota(jnp.int32, (out_ref.shape[0], feats_ref.shape[0]), 0)
    chosen = (pick_ref[...] == places).astype(BF)
    out_ref[...] = dot(chosen, feats_ref[...]).astype(BF)
    last = rows_ref.shape[1] - 128
    first = chunk - last
    codes_ref[...] = dot(chosen, rows_ref[:, last:]).T[first : first + 8, :]


def move_rows_kernel(pick_ref, rows_ref, out_ref):
    shape = (out_ref.shape[0], rows_ref.shape[0])
    places = lax.broadcasted_iota(jnp.int32, shape, 0)
    out_ref[...] = dot((pick_ref[...] == places).astype(BF), rows_ref[...])


def take_rows_kernel(pick_ref, rows_ref, out_ref):
    shape = (out_ref.shape[0], rows_ref.shape[0])
    places = lax.broadcasted_iota(jnp.int32, shape, 1)
    out_ref[...] = dot((pick_ref[...] == places).astype(BF), rows_ref[...]).astype(BF)


def embed_kernel(parts, mine_ref, text_ref, type_ref, pos_ref, gain_ref, bias_ref, *rest):
    pieces, (emb_ref, hid_ref, x_ref, xt_ref) = rest[:parts], rest[parts:]
    text_len = text_ref.shape[0]
    chunk = pieces[0].shape[1]
    types = type_ref[...].astype(F32)
    pos = pos_ref[...].astype(F32)
    emb_ref[:text_len, :] = text_ref[...].astype(F32) + types[0:1, :] + pos[:text_len, :]
    for k, piece in enumerate(pieces):
        for c in range(parts):

            @pl.when(mine_ref[0] ^ k == c)
            def _(piece=piece, c=c):
                at = slice(c * chunk, (c + 1) * chunk)
                emb_ref[text_len:, at] = piece[...].astype(F32)

    emb_ref[text_len:, :] += types[1:2, :] + pos[text_len:, :]
    hidden, _, _ = layer_norm(emb_ref[...], gain_ref[...], bias_ref[...])
    hid_ref[...] = hidden
    x_ref[...] = hidden.astype(BF)
    xt_ref[...] = x_ref[...].T


def embed_back_kernel(grad_ref, emb_ref, gain_ref, mid_ref, fin_ref, text_ref, reg_ref, vec):
    text_len = text_ref.shape[0]
    slots = emb_ref.shape[0] - text_len
    grad_in, gain_sum, bias_sum = norm_back(grad_ref[...], emb_ref[...], gain_ref[...])
    text_ref[...] = grad_in[:text_len, :].astype(BF)
    reg_ref[:slots, :] = grad_in[text_len:, :].astype(BF)
    vec[...] = jnp.zeros_like(vec)
    vec[0:1, :] = jnp.sum(grad_in[:text_len, :], axis=0, keepdims=True)
    vec[1:2, :] = jnp.sum(grad_in[text_len:, :], axis=0, keepdims=True)
    vec[2:3, :] = gain_sum
    vec[3:4, :] = bias_sum
    vec[4:6, :] = mid_ref[0:2, :]
    vec[6:8, :] = fin_ref[0:2, :]
    reg_ref[slots:, :] = vec[...].astype(BF)


def return_kernel(parts, mine_ref, pick_ref, feats_ref, codes_ref, w_ref, *rest):
    pieces = rest[:parts]
    wire_ref, proj_ref, box_ref, rest_ref, rows, columns, sums, full_ref = rest[parts:]
    slots = rows.shape[0] // parts
    chunk = columns.shape[1]
    for k in range(parts):
        rows[k * slots : (k + 1) * slots, :] = pieces[k][:slots, :]
    low = dot_nt(rows[...], w_ref[...]).astype(BF)
    places = lax.broadcasted_iota(jnp.int32, (wire_ref.shape[0], rows.shape[0]), 1)
    wire_ref[...] = dot((pick_ref[...] == places).astype(BF), low).astype(BF)
    full_ref[...] = dot(rows[...].T, feats_ref[...]).astype(BF)
    store_blocks(proj_ref, full_ref, mine_ref[1])
    sums[...] = pieces[0][...].astype(F32)
    for k in range(1, parts):
        sums[...] += pieces[k][...].astype(F32)

    def store_rows(value):
        columns[...] = value

    def store_rest(value):
        rest_ref[...] = value

    choose(mine_ref[0], parts, chunk, rows, store_rows)
    choose(mine_ref[0], parts, chunk, sums, store_rest)
    bins = box_ref.shape[1]
    codes = lax.broadcasted_iota(jnp.int32, (bins, rows.shape[0]), 0).astype(F32) + 1.0
    for c in range(box_ref.shape[0]):
        box_ref[c] = dot((codes_ref[c : c + 1, :] == codes).astype(BF), columns[...])


def text_kernel(parts, mine_ref, *rest):
    pieces, (out_ref, pos_ref, sums) = rest[:parts], rest[parts:]
    sums[...] = pieces[0][...].astype(F32)
    out_ref[mine_ref[0]] = sums[...]
    for k in range(1, parts):
        value = pieces[k][...].astype(F32)
        out_ref[mine_ref[0] ^ k] = value
        sums[...] += value

    def store(value):
        pos_ref[...] = value

    choose(mine_ref[0], parts, pos_ref.shape[1], sums, store)


def line_up_kernel(parts, mine_ref, *rest):
    pieces, out_ref = rest[:parts], rest[parts]
    for k in range(parts):
        out_ref[mine_ref[0] ^ k] = pieces[k][...]


def spread_kernel(parts, chunks_ref, out_ref):
    chunk = chunks_ref.shape[2]
    for c in range(parts):
        out_ref[:, c * chunk : (c + 1) * chunk] = chunks_ref[c]


def small_call(body, args, outs, scratch=(), scalar=False):
    specs = vmem_specs(len(args))
    if scalar:
        specs[0] = pl.BlockSpec(memory_space=pltpu.SMEM)
    got = call(body, outs, specs, vmem_specs(len(outs)), list(scratch), 1 << 20, 1 << 16)(*args)
    return got[0] if len(outs) == 1 else got


def swap(value, axis, bit):
    count = lax.axis_size(axis)
    return lax.ppermute(value, axis, [(i, i ^ bit) for i in range(count)])


def bits_of(axis):
    count = lax.axis_size(axis)
    return [1 << i for i in range(count.bit_length() - 1)]


def tie(first, second):
    return lax.optimization_barrier((first, second))


def after(value, first):
    return lax.optimization_barrier((value, first))[0]


def far_half(shard, bit):
    rows = shard.shape[0] // 2
    side = (lax.axis_index("dp") // bit) % 2
    return swap(lax.dynamic_slice_in_dim(shard, side * rows, rows, 0), "tensor", 2)


def gather_shards(shard, half, other):
    return [
        [shard],
        [swap(shard, "tensor", 1)],
        [half, other],
        [swap(half, "tensor", 1), swap(other, "tensor", 1)],
    ]


def pair_sum(terms):
    here = [terms[0], swap(terms[1], "tensor", 1)]
    return here, total([terms[2], swap(terms[3], "tensor", 1)]).astype(BF)


def total(summands):
    return sum(value.astype(F32) for value in summands)


def hop(values, bit):
    if values[0].ndim == 2:
        return values, None
    half = values[0].shape[0] // 2
    sent = total([v[half:] for v in values]).astype(BF)
    return [v[:half] for v in values], swap(sent, "dp", bit)


def finish(values, bits):
    if values[0].ndim == 2:
        term = total([v for v in values if v is not None]).astype(BF)
        term = term.reshape(lax.axis_size("dp"), -1, term.shape[1])
        return jnp.sum(lax.all_to_all(term, "dp", 0, 0, tiled=True).astype(F32), axis=0)
    for bit in bits:
        stay, come = hop(values, bit)
        values = stay + [come]
    return total(values)[0]


def local(
    text_embed,
    region_feats,
    box_coords,
    seg_ids,
    region_counts,
    send_index,
    recv_pos,
    w_proj,
    box_table,
    type_embed,
    pos_embed,
    gain_embed,
    bias_embed,
    w_qkv,
    w_mix,
    gain_mid,
    bias_mid,
    w_up,
    w_down,
    gain_final,
    bias_final,
    cotangent,
):
    parts = lax.axis_size("tensor")
    peers = lax.axis_size("dp")
    mine = lax.axis_index("tensor")
    dp_now = lax.axis_index("dp")
    mine_now = jnp.stack([mine, dp_now]).astype(jnp.int32)
    sides = jnp.stack([dp_now % 2, dp_now % 2, (dp_now // 2) % 2, dp_now]).astype(jnp.int32)
    row_count, text_len, width = text_embed.shape
    assert row_count == parts == 4
    length = seg_ids.shape[1]
    slots = length - text_len
    stored, depth = region_feats.shape
    capacity = send_index.shape[2]
    bins = box_table.shape[1]
    group = w_qkv.shape[2]
    heads = group // HD
    chunk = width // parts
    share = width // peers
    broad = -(-(chunk + 8) // 128) * 128
    wire = peers * capacity

    def own(array):
        return lax.dynamic_index_in_dim(array, mine, 0, keepdims=False)

    def line(vector):
        return vector.reshape(1, width)

    held = small_call(
        lambda *refs: project_kernel(parts, *refs),
        [mine_now, region_feats, w_proj],
        [((stored, chunk), F32 if k == 0 else BF) for k in range(parts)],
        [pltpu.VMEM((stored, width), F32)],
        scalar=True,
    )
    near = swap(held[1], "tensor", 1)
    across = (held[2].astype(F32) + swap(held[3], "tensor", 1).astype(F32)).astype(BF)

    across, (w_mix, w_qkv) = tie(across, (w_mix, w_qkv))
    far = swap(across, "tensor", 2)
    packed = small_call(pack_kernel, [w_mix, w_qkv], [((width, width), BF)])
    far, packed = tie(far, packed)
    att_half = far_half(packed, 1)

    send_flat = send_index.reshape(-1)
    recv_flat = recv_pos.reshape(-1)
    recv_slot = jnp.where(
        recv_flat >= 0,
        (recv_flat // length) * slots + recv_flat % length - text_len,
        -1,
    )
    recv_near = jnp.where(recv_flat >= 0, (recv_slot // slots ^ mine) * slots + recv_slot % slots, -1)
    near_line, near_column = recv_near.reshape(1, wire), recv_near.reshape(wire, 1)
    send_line, send_column = send_flat.reshape(1, wire), send_flat.reshape(wire, 1)
    outgoing = small_call(
        lambda *refs: outgoing_kernel(parts, *refs),
        [mine_now, held[0], near, far, box_coords, box_table, send_column],
        [((wire, broad), BF)],
        [pltpu.VMEM((stored, width), F32), pltpu.VMEM((stored, broad), BF)],
        scalar=True,
    )
    outgoing, w_up = tie(outgoing, w_up)
    up_half = far_half(w_up, 1)
    incoming = lax.all_to_all(
        outgoing.reshape(peers, capacity, broad), "dp", 0, 0, tiled=True
    ).reshape(wire, broad)
    allowed = key_mask(own(seg_ids), own(region_counts))
    incoming, (att_half, allow, allow_turned, text_mine) = tie(
        incoming, (att_half, allowed.astype(F32), allowed.T.astype(F32), own(text_embed))
    )
    att_other = swap(att_half, "dp", 1)
    placed = small_call(
        place_kernel, [near_line, incoming], [((slots, chunk), BF)] * row_count
    )
    placed = [swap(piece, "tensor", k) if k else piece for k, piece in enumerate(placed)]
    placed, w_down = tie(placed, w_down)
    down_half = far_half(w_down, 2)

    embedded, hidden0, inputs0, inputs0_turned = small_call(
        lambda *refs: embed_kernel(parts, *refs),
        [mine_now, text_mine, type_embed, pos_embed, line(gain_embed), line(bias_embed)] + placed,
        [
            ((length, width), F32),
            ((length, width), F32),
            ((length, width), BF),
            ((width, length), BF),
        ],
        scalar=True,
    )
    (hidden0, inputs0), feats = tie((hidden0, inputs0), region_feats)
    feats_wire = small_call(take_rows_kernel, [send_column, feats], [((wire, depth), BF)])
    feats_wire = lax.all_to_all(
        feats_wire.reshape(peers, capacity, depth), "dp", 0, 0, tiled=True
    ).reshape(wire, depth)
    (hidden0, inputs0), (up_half, att_other) = tie((hidden0, inputs0), (up_half, att_other))
    up_other = swap(up_half, "dp", 1)
    att_shards = gather_shards(packed, att_half, att_other)
    z, near_helds, near_lses = attend_call(heads, sides, inputs0, hidden0, allow, att_shards[:2])
    z, (up_other, down_half) = tie(z, (up_other, down_half))
    down_other = swap(down_half, "dp", 2)
    up = gather_shards(w_up, up_half, up_other)
    z, far_helds, far_lses = attend_call(heads, sides, inputs0, z, allow, att_shards[2:])
    helds, lses = near_helds + far_helds, near_lses + far_lses
    z, down_other = tie(z, down_other)
    down = gather_shards(w_down, down_half, down_other)
    slopes, down_terms, (final, x1t, grad_x2, grad_ffn, final_vectors) = forward_call(
        peers,
        sides,
        z,
        own(cotangent),
        line(gain_mid),
        line(bias_mid),
        line(gain_final),
        line(bias_final),
        up,
        down,
    )
    down_here, down_across = pair_sum(down_terms)
    final_far = swap(final, "tensor", 2)

    up_terms, (grad_x1, grad_attn, grad_attn_turned, mid_vectors) = backward_call(
        peers, sides, z, grad_x2, grad_ffn, x1t, line(gain_mid), up, down, slopes
    )
    (grad_attn, grad_x1), (down_across, final_far, feats_wire) = tie(
        (grad_attn, grad_x1), (down_across, final_far, feats_wire)
    )
    down_far = swap(down_across, "tensor", 2)
    up_here, up_across = pair_sum(up_terms)
    slot_feats, slot_codes = small_call(
        lambda *refs: place_feats_kernel(chunk, *refs),
        [near_line, incoming, feats_wire],
        [((row_count * slots, depth), BF), ((8, row_count * slots), F32)],
    )
    total0 = grad_x1
    att_terms = [None] * parts
    for at in (1, 0):
        picked = range(at, parts, 2)
        total0, terms = attend_back_call(
            heads,
            peers,
            sides,
            grad_attn,
            grad_attn_turned,
            inputs0_turned,
            total0,
            allow_turned,
            [att_shards[k] for k in picked],
            [helds[k] for k in picked],
            [lses[k] for k in picked],
        )
        for k, term in zip(picked, terms, strict=True):
            att_terms[k] = term
        if at:
            total0, (up_across, slot_feats) = tie(total0, (up_across, slot_feats))
            up_far = swap(up_across, "tensor", 2)
    total0, down_far = tie(total0, down_far)
    att_here, att_across = pair_sum(att_terms)

    def neighbours(piece, far):
        return [piece, swap(after(piece, far), "tensor", 1), far, swap(far, "tensor", 1)]

    text_own, regions_own = small_call(
        embed_back_kernel,
        [total0, embedded, line(gain_embed), mid_vectors, final_vectors],
        [((text_len, width), BF), ((slots + 16, width), BF)],
        [pltpu.VMEM((16, width), F32)],
    )
    regions_far = swap(regions_own, "tensor", 2)
    first_bit, *rest_bits = bits_of("dp")
    down_stay, down_come = hop(down_here + [down_far], first_bit)
    up_stay, up_come = hop(up_here + [up_far], first_bit)
    text_far = swap(after(text_own, regions_far), "tensor", 2)
    feats_back, proj_term, box_term, rest_sum = small_call(
        lambda *refs: return_kernel(parts, *refs),
        [mine_now, near_column, slot_feats, slot_codes, w_proj]
        + neighbours(regions_own, regions_far),
        [
            ((wire, depth), BF),
            (blocks_shape(peers, width, depth), BF),
            ((box_table.shape[0], bins, chunk), F32),
            ((slots + 16, chunk), F32),
        ],
        [
            pltpu.VMEM((row_count * slots, width), BF),
            pltpu.VMEM((row_count * slots, chunk), BF),
            pltpu.VMEM((slots + 16, width), F32),
            pltpu.VMEM((width, depth), BF),
        ],
        scalar=True,
    )
    att_far = swap(after(att_across, proj_term), "tensor", 2)
    proj_stay, proj_come = hop([proj_term], first_bit)
    feats_back = lax.all_to_all(
        feats_back.reshape(peers, capacity, depth), "dp", 0, 0, tiled=True
    ).reshape(wire, depth)
    feat_grad = small_call(move_rows_kernel, [send_line, feats_back], [((stored, depth), F32)])
    text_grad, text_sum = small_call(
        lambda *refs: text_kernel(parts, *refs),
        [mine_now] + neighbours(text_own, text_far),
        [((parts, text_len, width), F32), ((text_len, chunk), F32)],
        [pltpu.VMEM((text_len, width), F32)],
        scalar=True,
    )
    pos_term = jnp.concatenate([text_sum, rest_sum[:slots]], axis=0)
    bin_share = bins // peers
    pos_share = length // peers
    bundle = jnp.concatenate(
        [
            pos_term.reshape(peers, pos_share, chunk),
            box_term.reshape(-1, peers, bin_share, chunk)
            .transpose(1, 0, 2, 3)
            .reshape(peers, -1, chunk),
            jnp.broadcast_to(rest_sum[slots:], (peers, 16, chunk)),
        ],
        axis=1,
    ).astype(BF)
    grad_down = finish(down_stay + [down_come], rest_bits).T
    grad_up = finish(up_stay + [up_come], rest_bits)
    if proj_come is not None:
        proj_come = after(proj_come, text_sum)
    grad_proj = finish(proj_stay + [proj_come], rest_bits).T
    att_stay, att_come = hop(att_here + [att_far], first_bit)
    layer_output = small_call(
        lambda *refs: line_up_kernel(parts, *refs),
        [mine_now] + neighbours(final, after(final_far, bundle)),
        [((parts, length, width), BF)],
        scalar=True,
    )
    grad_att = finish(att_stay + [att_come], rest_bits)
    bundle = jnp.sum(
        lax.all_to_all(bundle, "dp", 0, 0, tiled=True).astype(F32), axis=0
    )
    bundle = lax.all_gather(bundle, "tensor", axis=0, tiled=False)
    bundle = small_call(
        lambda *refs: spread_kernel(parts, *refs), [bundle], [((bundle.shape[1], width), F32)]
    )
    grad_pos = bundle[:pos_share]
    grad_box = bundle[pos_share:-16].reshape(-1, bin_share, width)
    vectors = lax.dynamic_slice_in_dim(bundle[-16:], lax.axis_index("dp") * share, share, 1)

    grad_mix = grad_att[:, :group].T
    grad_qkv = grad_att[:, group:].reshape(share, 3, group).transpose(1, 0, 2)
    return (
        layer_output,
        text_grad,
        feat_grad,
        grad_proj,
        grad_box,
        vectors[:2],
        grad_pos,
        vectors[2],
        vectors[3],
        grad_qkv,
        grad_mix,
        vectors[4],
        vectors[5],
        grad_up,
        grad_down,
        vectors[6],
        vectors[7],
    )


def solution(mesh):
    return jax.shard_map(
        local,
        mesh=mesh,
        in_specs=(
            P("dp", None, None),
            P("dp", "tensor"),
            P("dp", None),
            P("dp", None),
            P("dp"),
            P("dp", None, None),
            P("dp", None, None),
            P("tensor", None),
            P(),
            P(),
            P(),
            P(),
            P(),
            P(None, None, "tensor"),
            P("tensor", None),
            P(),
            P(),
            P(None, "tensor"),
            P("tensor", None),
            P(),
            P(),
            P("dp", None, None),
        ),
        out_specs=(
            P("dp", None, None),
            P("dp", None, None),
            P("dp", "tensor"),
            P("tensor", "dp"),
            P(None, "dp", None),
            P(None, "dp"),
            P("dp", None),
            P("dp"),
            P("dp"),
            P(None, "dp", "tensor"),
            P("tensor", "dp"),
            P("dp"),
            P("dp"),
            P("dp", "tensor"),
            P("tensor", "dp"),
            P("dp"),
            P("dp"),
        ),
        check_vma=False,
    )
```
